32 devices in a mesh: energy: 8 (over z, x), slab: 4 (over y, core).
Axes of the slice: x: 2, y: 2, z: 4, core: 2. Of those that a mesh axis runs over, the one named last changes fastest.
Arguments:
- green: bfloat16 [256, 4608], P('energy', 'slab'), may hold values from -1.75 to 1.75
- sigma_in: bfloat16 [256, 4608], P('energy', 'slab'), may hold values from -6 to 6
- neighbours: int32 [32, 8], P('slab'), may hold values from 0 to 11
- coupling: float32 [32, 8], P('slab'), may hold values from 0.1 to 1
- send_down: int32 [4, 2], P('slab'), may hold values from 0 to 7, as said below
- send_up: int32 [4, 2], P('slab'), may hold values from 0 to 7, as said below
- offsets: int32 [16], replicated, may hold values from 1 to 32, as said below
- w_emit: float32 [16], replicated, may hold values from 0.02 to 0.2
- w_absorb: float32 [16], replicated, may hold values from 0.02 to 0.2
Outputs:
- sigma_ph: bfloat16 [256, 4608], P('energy', 'slab')
- g_less: bfloat16 [256, 4608], P('energy', 'slab')
The draws below stay inside these ranges and needn't reach their ends.
Inputs may be any that keep to these rules, and one draw needn't show every extreme that they name: Each row of send_down holds 2 distinct atom numbers of one slab. Each row of send_up holds 2 distinct atom numbers of one slab. The 16 offsets are distinct, and 32 is one of them.
All inputs are finite; a program needn't handle non-finite values.
Results may differ from the reference program's by a relative error of at most 0.0063.
Values may be sent and summed in bfloat16 or wider, within the bound.
A program may use at most 128 MiB of HBM per device.

```python
import math
import jax
import jax.numpy as jnp
from jax import lax

ORB = 12
NBRS = 8
FREQS = 16
PAIRS = 144
ENERGIES = 256
ATOMS_SLAB = 8
SLABS = 4
ATOMS = 32
HB = 2
MAXOFF = 32
N_SLAB = 4


def boundary_lists(key):
    keys = jax.random.split(key, SLABS)
    rows = [jax.random.permutation(keys[number], ATOMS_SLAB)[:HB] for number in range(SLABS)]
    return jnp.stack(rows).astype(jnp.int32)


def draw_send_down(key, part):
    return boundary_lists(jax.random.fold_in(key, 11))


def draw_send_up(key, part):
    return boundary_lists(jax.random.fold_in(key, 23))


def draw_offsets(key, part):
    first, second = jax.random.split(jax.random.fold_in(key, 37))
    chosen = jax.random.permutation(first, MAXOFF - 1)[:FREQS - 1] + 1
    values = jnp.concatenate([chosen.astype(jnp.int32), jnp.array([MAXOFF], jnp.int32)])
    return jax.random.permutation(second, values).astype(jnp.int32)


def plant(drawn, own_key, low, high):
    longest = drawn.shape.index(max(drawn.shape))
    spots = []
    for shift in (0, 1):
        where = [jax.random.randint(jax.random.fold_in(own_key, axis), (), 0, length) for axis, length in enumerate(drawn.shape)]
        where[longest] = (where[longest] + shift) % drawn.shape[longest]
        spots.append(tuple(where))
    return drawn.at[spots[0]].set(low).at[spots[1]].set(high)


def levels(rng, extent, cuts, low, top_value):
    level = 1.0
    for dim, shards_of in cuts:
        steps = jax.random.uniform(jax.random.fold_in(jax.random.fold_in(rng, 6), dim), (shards_of,), jnp.float32, low / len(cuts), top_value / len(cuts))
        level = level * jnp.repeat(jnp.exp(steps), extent[dim] // shards_of).reshape((-1,) + (1,) * (len(extent) - 1 - dim))
    return level


def centred(key, extent, width, limit, shards=(), kind=jnp.bfloat16):
    values = jax.random.normal(key, extent, jnp.float32) * width
    if len(shards) > 0:
        values = levels(key, extent, shards, -0.22, 0.18) * values
    return jnp.clip(values, min=-limit, max=limit).astype(kind)


def setup_inputs(seed: int = 0) -> dict:
    key_list = jax.random.split(jax.random.key(seed), 10)
    return {
        "green": centred(key_list[0], (ENERGIES, ATOMS * PAIRS), ORB ** -0.5, 1.75, ((0, 8), (1, 4))),
        "sigma_in": centred(key_list[1], (ENERGIES, ATOMS * PAIRS), 1.0, 6.0, ((0, 8), (1, 4))),
        "neighbours": plant(jax.random.randint(key_list[2], (ATOMS, NBRS), 0, ATOMS_SLAB + 2 * HB), jax.random.fold_in(key_list[2], 1), 0, (ATOMS_SLAB + 2 * HB) - 1).astype(jnp.int32),
        "coupling": jnp.clip(jnp.exp(math.log(1.0) - 2.3025851 * jax.random.uniform(key_list[3], (ATOMS, NBRS), jnp.float32) ** levels(key_list[3], (ATOMS, NBRS), ((0, 4),), -0.2, 0.2)), 0.1, 1.0),
        "send_down": draw_send_down(jax.random.fold_in(key_list[9], 71), 0),
        "send_up": draw_send_up(jax.random.fold_in(key_list[9], 71), 0),
        "offsets": draw_offsets(jax.random.fold_in(key_list[9], 71), 0),
        "w_emit": jnp.clip(jnp.exp(jax.random.uniform(key_list[7], (FREQS,), jnp.float32, math.log(0.02), math.log(0.2))), 0.02, 0.2),
        "w_absorb": jnp.clip(jnp.exp(jax.random.uniform(key_list[8], (FREQS,), jnp.float32, math.log(0.02), math.log(0.2))), 0.02, 0.2),
    }


def blocks(array):
    return array.astype(jnp.float32).reshape(array.shape[0], array.shape[1], ORB, ORB)


def sandwich(green, middle):
    left_side = blocks(green)
    product = jnp.einsum("eaij,eajk->eaik", left_side, middle, precision=lax.Precision.HIGHEST)
    result = jnp.einsum("eaik,ealk->eail", product, left_side, precision=lax.Precision.HIGHEST)
    return result.reshape(green.shape[0], green.shape[1], ORB * ORB)


def toeplitz(offsets, w_emit, w_absorb, count):
    positions = jnp.arange(count, dtype=jnp.int32)
    distance = positions[:, None] - positions[None, :]
    kernel = jnp.zeros((count, count), jnp.float32)
    for freq in range(offsets.shape[0]):
        kernel = kernel + w_emit[freq] * (distance == offsets[freq]).astype(jnp.float32)
        kernel = kernel + w_absorb[freq] * (distance == -offsets[freq]).astype(jnp.float32)
    return kernel.astype(jnp.bfloat16)


def reference(green, sigma_in, neighbours, coupling, send_down, send_up, offsets, w_emit, w_absorb):
    green = green.reshape(ENERGIES, ATOMS, PAIRS)
    sigma_in = sigma_in.reshape(ENERGIES, ATOMS, PAIRS)
    lesser = sandwich(green, blocks(sigma_in)).astype(jnp.bfloat16)
    kernel = toeplitz(offsets, w_emit, w_absorb, ENERGIES)
    pieces = []
    for slab_index in range(N_SLAB):
        start = slab_index * ATOMS_SLAB
        own = lesser[:, start:start + ATOMS_SLAB]
        if slab_index > 0:
            below = lesser[:, start - ATOMS_SLAB + send_up[slab_index - 1]]
        else:
            below = jnp.zeros((ENERGIES, HB, PAIRS), jnp.bfloat16)
        if slab_index < N_SLAB - 1:
            above = lesser[:, start + ATOMS_SLAB + send_down[slab_index + 1]]
        else:
            above = jnp.zeros((ENERGIES, HB, PAIRS), jnp.bfloat16)
        extended = jnp.concatenate([own, below, above], axis=1)
        total = jnp.zeros((ENERGIES, ATOMS_SLAB, PAIRS), jnp.float32)
        for column in range(NBRS):
            weights = coupling[start:start + ATOMS_SLAB, column]
            picked = extended[:, neighbours[start:start + ATOMS_SLAB, column]]
            total = total + weights[None, :, None] * picked.astype(jnp.float32)
        mixed = total.astype(jnp.bfloat16)
        sigma = jnp.dot(kernel, mixed.reshape(ENERGIES, ATOMS_SLAB * PAIRS), preferred_element_type=jnp.float32)
        pieces.append(sigma.astype(jnp.bfloat16).reshape(ENERGIES, ATOMS_SLAB, PAIRS))
    sigma_ph = jnp.concatenate(pieces, axis=1)
    combined = sigma_in.astype(jnp.float32) + sigma_ph.astype(jnp.float32)
    middle = combined.reshape(ENERGIES, ATOMS, ORB, ORB)
    g_less = sandwich(green, middle).astype(jnp.bfloat16)
    return sigma_ph.reshape(ENERGIES, ATOMS * PAIRS), g_less.reshape(ENERGIES, ATOMS * PAIRS)
```

```python
import functools

import jax
import jax.numpy as jnp
from jax import lax
from jax.experimental import pallas as pl
from jax.experimental.pallas import tpu as pltpu
from jax.sharding import PartitionSpec as P

ORB = 12
PADDED = 16
PAIRS = ORB * ORB
LANES = 128
MESH = pl.DeviceIdType.MESH
F32 = jnp.float32
BF16 = jnp.bfloat16


def iota(shape, dim):
    return lax.broadcasted_iota(jnp.int32, shape, dim)


def turned(matrix, block):
    return lax.dot_general(matrix, block, (((1,), (1,)), ((), ())), preferred_element_type=F32)


def dot(left, right):
    return jnp.dot(left, right, preferred_element_type=F32)


def each(count, body):
    if count <= 2:
        for index in range(count):
            body(index)
    else:
        lax.fori_loop(0, count, lambda index, carry: (body(index), carry)[1], 0)


def kernel(
    slabs, energies, rows, atoms, edge, nbrs, freqs,
    green_far, sigma_far, neighbours_far, coupling_far, down_far, up_far, offsets_far, emit_far, absorb_far,
    total, refreshed,
    green, sigma_in, neighbours, coupling, send_down, send_up, offsets, w_emit, w_absorb, fetched,
    plain, across, source, product, lesser, partial, mixing, outgoing, halo, band,
    edge_send, edge_recv, halo_send, halo_recv,
):
    per = LANES // rows
    groups = atoms // per
    edges = outgoing.shape[1]
    fetches = [
        pltpu.make_async_copy(far, near, fetched.at[place])
        for place, (far, near) in enumerate((
            (green_far, green), (sigma_far, sigma_in), (down_far, send_down), (up_far, send_up),
            (neighbours_far, neighbours), (coupling_far, coupling),
            (offsets_far, offsets), (emit_far, w_emit), (absorb_far, w_absorb),
        ))
    ]
    for fetch in fetches:
        fetch.start()
    my_slab = lax.axis_index("slab")
    my_energy = lax.axis_index("energy")
    barrier = pltpu.get_barrier_semaphore()
    links = (
        (my_slab > 0, {"slab": my_slab - 1}),
        (my_slab < slabs - 1, {"slab": my_slab + 1}),
        (my_energy > 0, {"energy": my_energy - 1}),
        (my_energy < energies - 1, {"energy": my_energy + 1}),
    )
    for there, target in links:
        @pl.when(there)
        def _():
            pl.semaphore_signal(barrier, inc=1, device_id=target, device_id_type=MESH)

    for side in range(2):
        @pl.when(jnp.logical_not(links[side][0]))
        def _():
            for block in range(edges):
                lesser[groups + side * edges + block] = jnp.zeros((PAIRS, LANES), BF16)

        @pl.when(jnp.logical_not(links[2 + side][0]))
        def _():
            for block in range(groups):
                halo[1 + side, block] = jnp.zeros((PAIRS, LANES), BF16)

    spread = (ORB * PADDED, PAIRS)
    high, low = iota(spread, 0) // PADDED, iota(spread, 0) % PADDED
    real = low < ORB
    straight = jnp.where(real & (iota(spread, 1) == high * ORB + low), 1.0, 0.0).astype(BF16)
    swapped = jnp.where(real & (iota(spread, 1) == low * ORB + high), 1.0, 0.0).astype(BF16)
    square = (LANES, LANES)
    same_energy = iota(square, 0) % rows == iota(square, 1) % rows
    lane_atom = iota((1, LANES), 1) // rows

    fetches[0].wait()
    fetches[1].wait()

    def gathered(ref, group):
        pieces = [
            ref[:, (group * per + atom) * PAIRS:(group * per + atom + 1) * PAIRS]
            for atom in range(per)
        ]
        return jnp.concatenate(pieces, axis=0)

    for group in range(groups):
        stacked = gathered(green, group)
        plain[group] = turned(straight, stacked).reshape(ORB, PADDED, LANES)
        across[group] = turned(swapped, stacked).reshape(ORB, PADDED, LANES)
        source[group] = turned(straight, gathered(sigma_in, group)).reshape(ORB, PADDED, LANES)

    def sandwich(group):
        for row in range(ORB):
            left = plain[group, row, 0:1, :] * source[group, 0]
            for inner in range(1, ORB):
                left = left + plain[group, row, inner:inner + 1, :] * source[group, inner]
            right = left[0:1, :] * across[group, 0]
            for inner in range(1, ORB):
                right = right + left[inner:inner + 1, :] * across[group, inner]
            product[group, row * ORB:(row + 1) * ORB, :] = right[:ORB, :]
        return product[group].astype(BF16)

    def first(group):
        lesser[group] = sandwich(group)

    each(groups, first)
    for fetch in fetches[2:]:
        fetch.wait()

    def lane_values(values):
        result = jnp.full((1, LANES), values[0])
        for place in range(1, len(values)):
            result = jnp.where(lane_atom == place, values[place], result)
        return result

    def expand(pieces):
        full = jnp.concatenate([jnp.broadcast_to(piece, (rows, LANES)) for piece in pieces], axis=0)
        return jnp.where(same_energy, full, 0.0).astype(BF16)

    for side, sent in ((0, send_down), (1, send_up)):
        for block in range(edges):
            first_slot = block * per
            wanted = lane_values(
                [sent[0, first_slot + t] if first_slot + t < edge else jnp.int32(-1) for t in range(per)]
            )
            chosen = jnp.zeros((PAIRS, LANES), F32)
            for group in range(groups):
                pieces = [
                    jnp.where(wanted == group * per + atom, 1.0, 0.0) for atom in range(per)
                ]
                chosen = chosen + dot(lesser[group], expand(pieces))
            outgoing[side, block] = chosen.astype(BF16)

    count = sum(there.astype(jnp.int32) for there, _ in links)
    pl.semaphore_wait(barrier, count)

    def edge_copy(side, block):
        return pltpu.make_async_remote_copy(
            src_ref=outgoing.at[side, block],
            dst_ref=lesser.at[groups + (1 - side) * edges + block],
            send_sem=edge_send.at[side, block],
            recv_sem=edge_recv.at[1 - side, block],
            device_id=links[side][1],
            device_id_type=MESH,
        )

    def arriving_edge(side, block):
        return pltpu.make_async_remote_copy(
            src_ref=outgoing.at[side, block],
            dst_ref=lesser.at[groups + side * edges + block],
            send_sem=edge_send.at[side, block],
            recv_sem=edge_recv.at[side, block],
            device_id=links[side][1],
            device_id_type=MESH,
        )

    def halo_copy(side, group):
        return pltpu.make_async_remote_copy(
            src_ref=halo.at[0, group],
            dst_ref=halo.at[2 - side, group],
            send_sem=halo_send.at[side],
            recv_sem=halo_recv.at[1 - side, group],
            device_id=links[2 + side][1],
            device_id_type=MESH,
        )

    def halo_sent(side):
        return pltpu.make_async_remote_copy(
            src_ref=halo.at[0],
            dst_ref=halo.at[2 - side],
            send_sem=halo_send.at[side],
            recv_sem=halo_recv.at[1 - side, 0],
            device_id=links[2 + side][1],
            device_id_type=MESH,
        )

    def arriving_halo(side, group):
        return pltpu.make_async_remote_copy(
            src_ref=halo.at[0, group],
            dst_ref=halo.at[1 + side, group],
            send_sem=halo_send.at[side],
            recv_sem=halo_recv.at[side, group],
            device_id=links[2 + side][1],
            device_id_type=MESH,
        )

    for side in range(2):
        @pl.when(links[side][0])
        def _():
            for block in range(edges):
                edge_copy(side, block).start()

    slots = -(-(atoms + 2 * edge) // 8) * 8
    blocks = groups + 2 * edges
    wide = 2 if groups % 2 == 0 else 1
    units = groups // wide

    def weigh(unit):
        for inner in range(wide):
            group = unit * wide + inner
            lanes = slice(inner * LANES, (inner + 1) * LANES)
            slot = iota((slots, LANES), 0)
            weights = jnp.zeros((slots, LANES), F32)
            for column in range(nbrs):
                atom_of = lane_values([neighbours[group * per + t, column] for t in range(per)])
                strength = lane_values([coupling[group * per + t, column] for t in range(per)])
                weights = weights + jnp.where(slot == atom_of, strength, 0.0)
            coarse = weights.astype(BF16).astype(F32)
            for level, part in enumerate((coarse, weights - coarse)):
                for block in range(blocks):
                    side = (block - groups) // edges
                    pieces = []
                    for t in range(per):
                        number = block * per + t if block < groups else ((block - groups) % edges) * per + t
                        at = number if block < groups else atoms + side * edge + number
                        known = block < groups or number < edge
                        pieces.append(part[at:at + 1, :] if known else jnp.zeros((1, LANES), F32))
                    mixing[unit, level, block, :, lanes] = expand(pieces)

    each(units, weigh)

    def joined(unit, first, last):
        value = None
        for start in range(first, last, 2):
            stop = min(start + 2, last)
            left = jnp.concatenate([lesser[block] for block in range(start, stop)], axis=1)
            for level in range(2):
                right = mixing[unit, level, start:stop].reshape((stop - start) * LANES, wide * LANES)
                term = dot(left, right)
                value = term if value is None else value + term
        return value

    def mix_own(unit):
        partial[unit] = joined(unit, 0, groups)

    each(units, mix_own)

    for side in range(2):
        @pl.when(links[side][0])
        def _():
            for block in range(edges):
                arriving_edge(side, block).wait_recv()

    def mix_border(unit):
        value = (partial[unit] + joined(unit, groups, blocks)).astype(BF16)
        for inner in range(wide):
            group = unit * wide + inner
            halo[0, group] = value[:, inner * LANES:(inner + 1) * LANES]
            for side in range(2):
                @pl.when(links[2 + side][0])
                def _():
                    halo_copy(side, group).start()

    each(units, mix_border)

    tall = (rows, LANES)
    same_atom = iota(square, 0) // rows == iota(square, 1) // rows
    for place, shift in enumerate((0, rows, -rows)):
        distance = iota(tall, 1) % rows - iota(tall, 0) + shift
        weight = jnp.zeros(tall, F32)
        for freq in range(freqs):
            weight = jnp.where(distance == offsets[freq], w_emit[freq], weight)
            weight = jnp.where(distance == -offsets[freq], w_absorb[freq], weight)
        full = jnp.concatenate([weight] * per, axis=0)
        full = jnp.where(same_atom, full, 0.0).astype(BF16)
        for inner in range(wide):
            for other in range(wide):
                band[place, inner * LANES:(inner + 1) * LANES, other * LANES:(other + 1) * LANES] = (
                    full if inner == other else jnp.zeros(square, BF16)
                )

    def neighbour(place, unit):
        return [halo[place, unit * wide + inner] for inner in range(wide)]

    def band_own(unit):
        partial[unit] = dot(jnp.concatenate(neighbour(0, unit), axis=1), band[0])

    each(units, band_own)

    def finish(unit):
        for inner in range(wide):
            group = unit * wide + inner
            for side in range(2):
                @pl.when(links[2 + side][0])
                def _():
                    arriving_halo(side, group).wait_recv()
            both = jnp.concatenate([halo[1, group], halo[2, group]], axis=1)
            sides = band[1:3, 0:LANES, 0:LANES].reshape(2 * LANES, LANES)
            value = partial[unit, :, inner * LANES:(inner + 1) * LANES] + dot(both, sides)
            total[group] = value.astype(BF16)
            product[group] = total[group].astype(F32)
            for row in range(ORB):
                source[group, row, 0:ORB, :] = (
                    source[group, row, 0:ORB, :] + product[group, row * ORB:(row + 1) * ORB, :]
                )
            refreshed[group] = sandwich(group)

    each(units, finish)

    for side in range(2):
        @pl.when(links[side][0])
        def _():
            for block in range(edges):
                edge_copy(side, block).wait_send()

        @pl.when(links[2 + side][0])
        def _():
            halo_sent(side).wait_send()


def finishing(rows, total, refreshed, sigma_out, g_out, sigma_near, g_near, written):
    per = LANES // rows
    square = (LANES, LANES)
    identity = jnp.where(iota(square, 0) == iota(square, 1), 1.0, 0.0).astype(BF16)
    copies = []
    for place, (values, near, out) in enumerate(((total, sigma_near, sigma_out), (refreshed, g_near, g_out))):
        for group in range(total.shape[0]):
            back = turned(identity, values[group]).astype(BF16)
            for atom in range(per):
                at = (group * per + atom) * PAIRS
                near[:, at:at + PAIRS] = back[atom * rows:(atom + 1) * rows, :]
        copies.append(pltpu.make_async_copy(near, out, written.at[place]))
        copies[-1].start()
    for copy in copies:
        copy.wait()


def compact(
    slabs, energies, rows, atoms, edge, nbrs, freqs,
    green_far, sigma_far, neighbours_far, coupling_far, down_far, up_far, offsets_far, emit_far, absorb_far,
    sigma_near, g_near,
    green, sigma_in, neighbours, coupling, send_down, send_up, offsets, w_emit, w_absorb, fetched,
    cut, across, source, product, lesser, partial, mixing, border, outgoing, arrived, halo, own_band, far_band,
    edge_send, edge_recv, halo_send, halo_recv, relay_send,
):
    per = LANES // rows
    groups = atoms // per
    last = groups - 1
    half = PAIRS // 2
    middle = LANES // 2
    span = groups * LANES
    fetches = [
        pltpu.make_async_copy(far, near, fetched.at[place])
        for place, (far, near) in enumerate((
            (green_far, green), (sigma_far, sigma_in), (down_far, send_down), (up_far, send_up),
            (neighbours_far, neighbours), (coupling_far, coupling),
            (offsets_far, offsets), (emit_far, w_emit), (absorb_far, w_absorb),
        ))
    ]
    for fetch in fetches:
        fetch.start()
    my_slab = lax.axis_index("slab")
    my_energy = lax.axis_index("energy")
    ahead = 1 - 2 * (my_energy % 2)
    relayed = my_slab == slabs - 1
    beyond = my_energy - ahead
    inside = (beyond >= 0) & (beyond < energies)
    onward, origin = my_energy + 2 * ahead, my_energy - 2 * ahead
    relays = relayed & (onward >= 0) & (onward < energies)
    barrier = pltpu.get_barrier_semaphore()
    links = (
        (my_slab > 0, {"slab": my_slab - 1}),
        (my_slab < slabs - 1, {"slab": my_slab + 1}),
        (my_energy >= 0, {"energy": my_energy + ahead}),
        (inside, {"energy": beyond}),
        (relays, {"energy": onward}),
        (relayed & inside, {"energy": origin}),
    )
    for there, target in links:
        @pl.when(there)
        def _():
            pl.semaphore_signal(barrier, inc=1, device_id=target, device_id_type=MESH)

    for side in range(2):
        @pl.when(jnp.logical_not(links[side][0]))
        def _():
            arrived[side] = jnp.zeros((half, LANES), BF16)

    @pl.when(jnp.logical_not(inside))
    def _():
        for group in range(groups):
            halo[2, group] = jnp.zeros((PAIRS, LANES), BF16)

    spread = (ORB * PADDED, PAIRS)
    high, low = iota(spread, 0) // PADDED, iota(spread, 0) % PADDED
    swapped = jnp.where((low < ORB) & (iota(spread, 1) == low * ORB + high), 1.0, 0.0).astype(BF16)
    compacted = (PAIRS, PAIRS)
    straight = jnp.where(iota(compacted, 0) == iota(compacted, 1), 1.0, 0.0).astype(BF16)
    square = (LANES, LANES)

    def load(slot, blocks):
        stacked = jnp.concatenate([cut[0, block] for block in blocks], axis=0)
        across[slot] = turned(swapped, stacked).reshape(ORB, PADDED, LANES)
        stacked = jnp.concatenate([cut[1, block] for block in blocks], axis=0)
        source[slot] = turned(straight, stacked)

    def sandwich(slot):
        columns = []
        for column in range(ORB):
            left = across[slot, 0] * source[slot, column:column + 1, :]
            for inner in range(1, ORB):
                at = inner * ORB + column
                left = left + across[slot, inner] * source[slot, at:at + 1, :]
            columns.append(left)
        for column in range(ORB):
            right = columns[0] * across[slot, 0, column:column + 1, :]
            for inner in range(1, ORB):
                right = right + columns[inner] * across[slot, inner, column:column + 1, :]
            product[slot, pl.ds(column, ORB, stride=ORB), :] = right[:ORB, :]
        return product[slot]

    for fetch in fetches[:4]:
        fetch.wait()
    for place, ref in enumerate((green, sigma_in)):
        for atom in range(atoms):
            cut[place, atom] = ref[:, atom * PAIRS:(atom + 1) * PAIRS]

    load(groups, [send_down[0, t] for t in range(edge)] + [send_up[0, t] for t in range(edge)])
    edges = sandwich(groups)
    top, bottom = edges[:half], edges[half:]
    lower = iota((half, LANES), 1) < middle
    outgoing[0] = jnp.where(lower, top, pltpu.roll(bottom, middle, 1)).astype(BF16)
    outgoing[1] = jnp.where(lower, pltpu.roll(top, middle, 1), bottom).astype(BF16)

    count = sum(there.astype(jnp.int32) for there, _ in links)
    pl.semaphore_wait(barrier, count)

    def edge_copy(side, slot):
        return pltpu.make_async_remote_copy(
            src_ref=outgoing.at[side],
            dst_ref=arrived.at[slot],
            send_sem=edge_send.at[side],
            recv_sem=edge_recv.at[slot],
            device_id=links[side][1],
            device_id_type=MESH,
        )

    def halo_copy(kind, group):
        return pltpu.make_async_remote_copy(
            src_ref=halo.at[0, group],
            dst_ref=halo.at[1 + kind, group],
            send_sem=halo_send.at[kind, group],
            recv_sem=halo_recv.at[kind, group],
            device_id=links[2 + kind][1],
            device_id_type=MESH,
        )

    def relay_copy():
        return pltpu.make_async_remote_copy(
            src_ref=halo.at[1, last],
            dst_ref=halo.at[2, last],
            send_sem=relay_send,
            recv_sem=halo_recv.at[1, last],
            device_id=links[4][1],
            device_id_type=MESH,
        )

    for side in range(2):
        @pl.when(links[side][0])
        def _():
            edge_copy(side, 1 - side).start()

    for group in range(groups):
        load(group, range(group * per, (group + 1) * per))
    for group in range(groups):
        lesser[:, group * LANES:(group + 1) * LANES] = sandwich(group).astype(BF16)

    for fetch in fetches[4:]:
        fetch.wait()
    slots = -(-(atoms + 2 * edge) // 8) * 8
    lane_atom = iota((1, span), 1) // rows

    def lane_values(values):
        result = jnp.full((1, span), values[0])
        for place in range(1, len(values)):
            result = jnp.where(lane_atom == place, values[place], result)
        return result

    slot_of = iota((slots, span), 0)
    weights = jnp.zeros((slots, span), F32)
    for column in range(nbrs):
        atom_of = lane_values([neighbours[atom, column] for atom in range(atoms)])
        strength = lane_values([coupling[atom, column] for atom in range(atoms)])
        weights = weights + jnp.where(slot_of == atom_of, strength, 0.0)
    tall = (rows, span)
    same_energy = iota(tall, 0) == iota(tall, 1) % rows

    def expanded(at):
        return jnp.where(same_energy, jnp.broadcast_to(weights[at:at + 1, :], tall), 0.0).astype(BF16)

    for atom in range(atoms):
        mixing[atom * rows:(atom + 1) * rows, :] = expanded(atom)
    empty = jnp.zeros((middle, span), BF16)
    for side in range(2):
        start = side * LANES
        for t in range(edge):
            part = expanded(atoms + side * edge + t)
            border[start + t * rows:start + (t + 1) * rows, 0:span] = part
            border[start + middle + t * rows:start + middle + (t + 1) * rows, span:2 * span] = part
        border[start:start + middle, span:2 * span] = empty
        border[start + middle:start + LANES, 0:span] = empty

    partial[...] = dot(lesser[...], mixing[...])

    for side in range(2):
        @pl.when(links[side][0])
        def _():
            edge_copy(side, side).wait_recv()

    crossing = dot(jnp.concatenate([arrived[0], arrived[1]], axis=1), border[...])
    crossing = jnp.concatenate([crossing[:, 0:span], crossing[:, span:2 * span]], axis=0)
    mixed = (partial[...] + crossing).astype(BF16)
    for group in range(groups):
        halo[0, group] = mixed[:, group * LANES:(group + 1) * LANES]

    direct = jnp.logical_not(relayed)

    @pl.when(relayed)
    def _():
        halo_copy(0, last).start()

    for group in range(groups):
        @pl.when(inside if group < last else inside & direct)
        def _():
            halo_copy(1, group).start()

        if group < last:
            halo_copy(0, group).start()

    @pl.when(direct)
    def _():
        halo_copy(0, last).start()

    same_atom = iota(square, 0) // rows == iota(square, 1) // rows
    narrow = (rows, LANES)
    distance = iota(narrow, 1) % rows - iota(narrow, 0)
    near_weight = jnp.zeros(narrow, F32)
    ahead_weight = jnp.zeros(narrow, F32)
    behind_weight = jnp.zeros(narrow, F32)
    ahead_gap = rows - ahead * distance
    behind_gap = rows + ahead * distance
    upward = ahead > 0
    for freq in range(freqs):
        offset, emit, absorb = offsets[freq], w_emit[freq], w_absorb[freq]
        near_weight = jnp.where(distance == offset, emit, near_weight)
        near_weight = jnp.where(distance == -offset, absorb, near_weight)
        ahead_weight = jnp.where(ahead_gap == offset, jnp.where(upward, absorb, emit), ahead_weight)
        behind_weight = jnp.where(behind_gap == offset, jnp.where(upward, emit, absorb), behind_weight)

    def band(weight):
        return jnp.where(same_atom, jnp.concatenate([weight] * per, axis=0), 0.0).astype(BF16)

    own_band[...] = band(near_weight)
    far_band[0:LANES, :] = band(ahead_weight)
    far_band[LANES:2 * LANES, :] = band(behind_weight)
    for group in range(groups):
        partial[:, group * LANES:(group + 1) * LANES] = dot(halo[0, group], own_band[...])

    @pl.when(relayed)
    def _():
        halo_copy(0, last).wait_recv()

    @pl.when(relays)
    def _():
        relay_copy().start()

    identity = jnp.where(iota(square, 0) == iota(square, 1), 1.0, 0.0).astype(BF16)

    def place_rows(near, group, values):
        back = turned(identity, values).astype(BF16)
        for atom in range(per):
            at = (group * per + atom) * PAIRS
            near[:, at:at + PAIRS] = back[atom * rows:(atom + 1) * rows, :]

    for group in range(groups):
        if group < last:
            halo_copy(0, group).wait_recv()
        else:
            @pl.when(direct)
            def _():
                halo_copy(0, last).wait_recv()

        @pl.when(inside)
        def _():
            halo_copy(1, group).wait_recv()

        both = jnp.concatenate([halo[1, group], halo[2, group]], axis=1)
        value = partial[:, group * LANES:(group + 1) * LANES] + dot(both, far_band[...])
        total = value.astype(BF16)
        place_rows(sigma_near, group, total)
        source[group] = source[group] + total.astype(F32)
        place_rows(g_near, group, sandwich(group).astype(BF16))

    for side in range(2):
        @pl.when(links[side][0])
        def _():
            edge_copy(side, 1 - side).wait_send()

    for group in range(groups):
        halo_copy(0, group).wait_send()

        @pl.when(inside if group < last else inside & direct)
        def _():
            halo_copy(1, group).wait_send()

    @pl.when(relays)
    def _():
        relay_copy().wait_send()


def delivering(sigma_near, g_near, sigma_out, g_out, written):
    copies = [
        pltpu.make_async_copy(near, out, written.at[place])
        for place, (near, out) in enumerate(((sigma_near, sigma_out), (g_near, g_out)))
    ]
    for copy in copies:
        copy.start()
    for copy in copies:
        copy.wait()


def on_device_compact(slabs, energies, green, sigma_in, *smalls):
    rows, flat = green.shape
    atoms = flat // PAIRS
    neighbours, _, send_down, _, offsets, _, _ = smalls
    edge = send_down.shape[1]
    per = LANES // rows
    groups = atoms // per
    span = groups * LANES
    vmem = pl.BlockSpec(memory_space=pltpu.VMEM)
    far = pl.BlockSpec(memory_space=pltpu.HBM)
    body = functools.partial(
        compact, slabs, energies, rows, atoms, edge, neighbours.shape[1], offsets.shape[0]
    )
    shape = jax.ShapeDtypeStruct((rows, flat), BF16)
    near_shape = pltpu.VMEM((rows, flat), BF16)
    near = pl.pallas_call(
        body,
        out_shape=(near_shape, near_shape),
        in_specs=[far] * 9,
        out_specs=(vmem, vmem),
        scratch_shapes=[
            pltpu.VMEM(green.shape, BF16),
            pltpu.VMEM(green.shape, BF16),
            *[pltpu.SMEM(small.shape, small.dtype) for small in smalls],
            pltpu.SemaphoreType.DMA((9,)),
            pltpu.VMEM((2, atoms, rows, PAIRS), BF16),
            pltpu.VMEM((groups + 1, ORB, PADDED, LANES), F32),
            pltpu.VMEM((groups + 1, PAIRS, LANES), F32),
            pltpu.VMEM((groups + 1, PAIRS, LANES), F32),
            pltpu.VMEM((PAIRS, span), BF16),
            pltpu.VMEM((PAIRS, span), F32),
            pltpu.VMEM((span, span), BF16),
            pltpu.VMEM((2 * LANES, 2 * span), BF16),
            pltpu.VMEM((2, PAIRS // 2, LANES), BF16),
            pltpu.VMEM((2, PAIRS // 2, LANES), BF16),
            pltpu.VMEM((3, groups, PAIRS, LANES), BF16),
            pltpu.VMEM((LANES, LANES), BF16),
            pltpu.VMEM((2 * LANES, LANES), BF16),
            pltpu.SemaphoreType.DMA((2,)),
            pltpu.SemaphoreType.DMA((2,)),
            pltpu.SemaphoreType.DMA((2, groups)),
            pltpu.SemaphoreType.DMA((2, groups)),
            pltpu.SemaphoreType.DMA,
        ],
        compiler_params=pltpu.CompilerParams(
            collective_id=0, has_side_effects=True
        ),
    )(green, sigma_in, *smalls)
    return pl.pallas_call(
        delivering,
        out_shape=(shape, shape),
        in_specs=[vmem] * 2,
        out_specs=(far, far),
        scratch_shapes=[pltpu.SemaphoreType.DMA((2,))],
        compiler_params=pltpu.CompilerParams(vmem_limit_bytes=(4 + groups) << 20),
    )(*near)


def on_device(slabs, energies, green, sigma_in, neighbours, coupling, send_down, send_up, offsets, w_emit, w_absorb):
    rows, flat = green.shape
    atoms = flat // PAIRS
    edge = send_down.shape[1]
    per = LANES // rows
    groups = atoms // per
    edges = -(-edge // per)
    wide = 2 if groups % 2 == 0 else 1
    smalls = (neighbours, coupling, send_down, send_up, offsets, w_emit, w_absorb)
    if 2 * edge == per and groups == 2 and energies % 2 == 0:
        return on_device_compact(slabs, energies, green, sigma_in, *smalls)
    vmem = pl.BlockSpec(memory_space=pltpu.VMEM)
    far = pl.BlockSpec(memory_space=pltpu.HBM)
    body = functools.partial(
        kernel, slabs, energies, rows, atoms, edge, neighbours.shape[1], offsets.shape[0]
    )
    shape = jax.ShapeDtypeStruct((rows, flat), BF16)
    turned_shape = pltpu.VMEM((groups, PAIRS, LANES), BF16)
    total, refreshed = pl.pallas_call(
        body,
        out_shape=(turned_shape, turned_shape),
        in_specs=[far] * 9,
        out_specs=(vmem, vmem),
        scratch_shapes=[
            pltpu.VMEM(green.shape, BF16),
            pltpu.VMEM(green.shape, BF16),
            *[pltpu.SMEM(small.shape, small.dtype) for small in smalls],
            pltpu.SemaphoreType.DMA((9,)),
            pltpu.VMEM((groups, ORB, PADDED, LANES), F32),
            pltpu.VMEM((groups, ORB, PADDED, LANES), F32),
            pltpu.VMEM((groups, ORB, PADDED, LANES), F32),
            pltpu.VMEM((groups, PAIRS, LANES), F32),
            pltpu.VMEM((groups + 2 * edges, PAIRS, LANES), BF16),
            pltpu.VMEM((groups // wide, PAIRS, wide * LANES), F32),
            pltpu.VMEM((groups // wide, 2, groups + 2 * edges, LANES, wide * LANES), BF16),
            pltpu.VMEM((2, edges, PAIRS, LANES), BF16),
            pltpu.VMEM((3, groups, PAIRS, LANES), BF16),
            pltpu.VMEM((3, wide * LANES, wide * LANES), BF16),
            pltpu.SemaphoreType.DMA((2, edges)),
            pltpu.SemaphoreType.DMA((2, edges)),
            pltpu.SemaphoreType.DMA((2,)),
            pltpu.SemaphoreType.DMA((2, groups)),
        ],
        compiler_params=pltpu.CompilerParams(
            collective_id=0, has_side_effects=True
        ),
    )(green, sigma_in, *smalls)
    return pl.pallas_call(
        functools.partial(finishing, rows),
        out_shape=(shape, shape),
        in_specs=[vmem] * 2,
        out_specs=(far, far),
        scratch_shapes=[
            pltpu.VMEM((rows, flat), BF16),
            pltpu.VMEM((rows, flat), BF16),
            pltpu.SemaphoreType.DMA((2,)),
        ],
        compiler_params=pltpu.CompilerParams(vmem_limit_bytes=(4 + groups) << 20),
    )(total, refreshed)


def solution(mesh):
    placed = (
        P("energy", "slab"),
        P("energy", "slab"),
        P("slab", None),
        P("slab", None),
        P("slab", None),
        P("slab", None),
        P(),
        P(),
        P(),
    )
    return jax.shard_map(
        functools.partial(on_device, mesh.shape["slab"], mesh.shape["energy"]),
        mesh=mesh,
        in_specs=placed,
        out_specs=(P("energy", "slab"), P("energy", "slab")),
        check_vma=False,
    )
```

```python
import functools

import jax
import jax.numpy as jnp
from jax import lax
from jax.experimental import pallas as pl
from jax.experimental.pallas import tpu as pltpu
from jax.sharding import PartitionSpec as P

ORB = 12
PADDED = 16
PAIRS = ORB * ORB
LANES = 128
MESH = pl.DeviceIdType.MESH
F32 = jnp.float32
BF16 = jnp.bfloat16


def iota(shape, dim):
    return lax.broadcasted_iota(jnp.int32, shape, dim)


def turned(matrix, block):
    return lax.dot_general(matrix, block, (((1,), (1,)), ((), ())), preferred_element_type=F32)


def dot(left, right):
    return jnp.dot(left, right, preferred_element_type=F32)


def each(count, body):
    if count <= 2:
        for index in range(count):
            body(index)
    else:
        lax.fori_loop(0, count, lambda index, carry: (body(index), carry)[1], 0)


def kernel(
    slabs, energies, rows, atoms, edge, nbrs, freqs,
    green_far, sigma_far, neighbours_far, coupling_far, down_far, up_far, offsets_far, emit_far, absorb_far,
    total, refreshed,
    green, sigma_in, neighbours, coupling, send_down, send_up, offsets, w_emit, w_absorb, fetched,
    plain, across, source, product, lesser, partial, mixing, outgoing, halo, band,
    edge_send, edge_recv, halo_send, halo_recv,
):
    per = LANES // rows
    groups = atoms // per
    edges = outgoing.shape[1]
    fetches = [
        pltpu.make_async_copy(far, near, fetched.at[place])
        for place, (far, near) in enumerate((
            (green_far, green), (sigma_far, sigma_in), (down_far, send_down), (up_far, send_up),
            (neighbours_far, neighbours), (coupling_far, coupling),
            (offsets_far, offsets), (emit_far, w_emit), (absorb_far, w_absorb),
        ))
    ]
    for fetch in fetches:
        fetch.start()
    my_slab = lax.axis_index("slab")
    my_energy = lax.axis_index("energy")
    barrier = pltpu.get_barrier_semaphore()
    links = (
        (my_slab > 0, {"slab": my_slab - 1}),
        (my_slab < slabs - 1, {"slab": my_slab + 1}),
        (my_energy > 0, {"energy": my_energy - 1}),
        (my_energy < energies - 1, {"energy": my_energy + 1}),
    )
    for there, target in links:
        @pl.when(there)
        def _():
            pl.semaphore_signal(barrier, inc=1, device_id=target, device_id_type=MESH)

    for side in range(2):
        @pl.when(jnp.logical_not(links[side][0]))
        def _():
            for block in range(edges):
                lesser[groups + side * edges + block] = jnp.zeros((PAIRS, LANES), BF16)

        @pl.when(jnp.logical_not(links[2 + side][0]))
        def _():
            for block in range(groups):
                halo[1 + side, block] = jnp.zeros((PAIRS, LANES), BF16)

    spread = (ORB * PADDED, PAIRS)
    high, low = iota(spread, 0) // PADDED, iota(spread, 0) % PADDED
    real = low < ORB
    straight = jnp.where(real & (iota(spread, 1) == high * ORB + low), 1.0, 0.0).astype(BF16)
    swapped = jnp.where(real & (iota(spread, 1) == low * ORB + high), 1.0, 0.0).astype(BF16)
    square = (LANES, LANES)
    same_energy = iota(square, 0) % rows == iota(square, 1) % rows
    lane_atom = iota((1, LANES), 1) // rows

    fetches[0].wait()
    fetches[1].wait()

    def gathered(ref, group):
        pieces = [
            ref[:, (group * per + atom) * PAIRS:(group * per + atom + 1) * PAIRS]
            for atom in range(per)
        ]
        return jnp.concatenate(pieces, axis=0)

    for group in range(groups):
        stacked = gathered(green, group)
        plain[group] = turned(straight, stacked).reshape(ORB, PADDED, LANES)
        across[group] = turned(swapped, stacked).reshape(ORB, PADDED, LANES)
        source[group] = turned(straight, gathered(sigma_in, group)).reshape(ORB, PADDED, LANES)

    def sandwich(group):
        for row in range(ORB):
            left = plain[group, row, 0:1, :] * source[group, 0]
            for inner in range(1, ORB):
                left = left + plain[group, row, inner:inner + 1, :] * source[group, inner]
            right = left[0:1, :] * across[group, 0]
            for inner in range(1, ORB):
                right = right + left[inner:inner + 1, :] * across[group, inner]
            product[group, row * ORB:(row + 1) * ORB, :] = right[:ORB, :]
        return product[group].astype(BF16)

    def first(group):
        lesser[group] = sandwich(group)

    each(groups, first)
    for fetch in fetches[2:]:
        fetch.wait()

    def lane_values(values):
        result = jnp.full((1, LANES), values[0])
        for place in range(1, len(values)):
            result = jnp.where(lane_atom == place, values[place], result)
        return result

    def expand(pieces):
        full = jnp.concatenate([jnp.broadcast_to(piece, (rows, LANES)) for piece in pieces], axis=0)
        return jnp.where(same_energy, full, 0.0).astype(BF16)

    for side, sent in ((0, send_down), (1, send_up)):
        for block in range(edges):
            first_slot = block * per
            wanted = lane_values(
                [sent[0, first_slot + t] if first_slot + t < edge else jnp.int32(-1) for t in range(per)]
            )
            chosen = jnp.zeros((PAIRS, LANES), F32)
            for group in range(groups):
                pieces = [
                    jnp.where(wanted == group * per + atom, 1.0, 0.0) for atom in range(per)
                ]
                chosen = chosen + dot(lesser[group], expand(pieces))
            outgoing[side, block] = chosen.astype(BF16)

    count = sum(there.astype(jnp.int32) for there, _ in links)
    pl.semaphore_wait(barrier, count)

    def edge_copy(side, block):
        return pltpu.make_async_remote_copy(
            src_ref=outgoing.at[side, block],
            dst_ref=lesser.at[groups + (1 - side) * edges + block],
            send_sem=edge_send.at[side, block],
            recv_sem=edge_recv.at[1 - side, block],
            device_id=links[side][1],
            device_id_type=MESH,
        )

    def arriving_edge(side, block):
        return pltpu.make_async_remote_copy(
            src_ref=outgoing.at[side, block],
            dst_ref=lesser.at[groups + side * edges + block],
            send_sem=edge_send.at[side, block],
            recv_sem=edge_recv.at[side, block],
            device_id=links[side][1],
            device_id_type=MESH,
        )

    def halo_copy(side, group):
        return pltpu.make_async_remote_copy(
            src_ref=halo.at[0, group],
            dst_ref=halo.at[2 - side, group],
            send_sem=halo_send.at[side],
            recv_sem=halo_recv.at[1 - side, group],
            device_id=links[2 + side][1],
            device_id_type=MESH,
        )

    def halo_sent(side):
        return pltpu.make_async_remote_copy(
            src_ref=halo.at[0],
            dst_ref=halo.at[2 - side],
            send_sem=halo_send.at[side],
            recv_sem=halo_recv.at[1 - side, 0],
            device_id=links[2 + side][1],
            device_id_type=MESH,
        )

    def arriving_halo(side, group):
        return pltpu.make_async_remote_copy(
            src_ref=halo.at[0, group],
            dst_ref=halo.at[1 + side, group],
            send_sem=halo_send.at[side],
            recv_sem=halo_recv.at[side, group],
            device_id=links[2 + side][1],
            device_id_type=MESH,
        )

    for side in range(2):
        @pl.when(links[side][0])
        def _():
            for block in range(edges):
                edge_copy(side, block).start()

    slots = -(-(atoms + 2 * edge) // 8) * 8
    blocks = groups + 2 * edges
    wide = 2 if groups % 2 == 0 else 1
    units = groups // wide

    def weigh(unit):
        for inner in range(wide):
            group = unit * wide + inner
            lanes = slice(inner * LANES, (inner + 1) * LANES)
            slot = iota((slots, LANES), 0)
            weights = jnp.zeros((slots, LANES), F32)
            for column in range(nbrs):
                atom_of = lane_values([neighbours[group * per + t, column] for t in range(per)])
                strength = lane_values([coupling[group * per + t, column] for t in range(per)])
                weights = weights + jnp.where(slot == atom_of, strength, 0.0)
            coarse = weights.astype(BF16).astype(F32)
            for level, part in enumerate((coarse, weights - coarse)):
                for block in range(blocks):
                    side = (block - groups) // edges
                    pieces = []
                    for t in range(per):
                        number = block * per + t if block < groups else ((block - groups) % edges) * per + t
                        at = number if block < groups else atoms + side * edge + number
                        known = block < groups or number < edge
                        pieces.append(part[at:at + 1, :] if known else jnp.zeros((1, LANES), F32))
                    mixing[unit, level, block, :, lanes] = expand(pieces)

    each(units, weigh)

    def joined(unit, first, last):
        value = None
        for start in range(first, last, 2):
            stop = min(start + 2, last)
            left = jnp.concatenate([lesser[block] for block in range(start, stop)], axis=1)
            for level in range(2):
                right = mixing[unit, level, start:stop].reshape((stop - start) * LANES, wide * LANES)
                term = dot(left, right)
                value = term if value is None else value + term
        return value

    def mix_own(unit):
        partial[unit] = joined(unit, 0, groups)

    each(units, mix_own)

    for side in range(2):
        @pl.when(links[side][0])
        def _():
            for block in range(edges):
                arriving_edge(side, block).wait_recv()

    def mix_border(unit):
        value = (partial[unit] + joined(unit, groups, blocks)).astype(BF16)
        for inner in range(wide):
            group = unit * wide + inner
            halo[0, group] = value[:, inner * LANES:(inner + 1) * LANES]
            for side in range(2):
                @pl.when(links[2 + side][0])
                def _():
                    halo_copy(side, group).start()

    each(units, mix_border)

    tall = (rows, LANES)
    same_atom = iota(square, 0) // rows == iota(square, 1) // rows
    for place, shift in enumerate((0, rows, -rows)):
        distance = iota(tall, 1) % rows - iota(tall, 0) + shift
        weight = jnp.zeros(tall, F32)
        for freq in range(freqs):
            weight = jnp.where(distance == offsets[freq], w_emit[freq], weight)
            weight = jnp.where(distance == -offsets[freq], w_absorb[freq], weight)
        full = jnp.concatenate([weight] * per, axis=0)
        full = jnp.where(same_atom, full, 0.0).astype(BF16)
        for inner in range(wide):
            for other in range(wide):
                band[place, inner * LANES:(inner + 1) * LANES, other * LANES:(other + 1) * LANES] = (
                    full if inner == other else jnp.zeros(square, BF16)
                )

    def neighbour(place, unit):
        return [halo[place, unit * wide + inner] for inner in range(wide)]

    def band_own(unit):
        partial[unit] = dot(jnp.concatenate(neighbour(0, unit), axis=1), band[0])

    each(units, band_own)

    def finish(unit):
        for inner in range(wide):
            group = unit * wide + inner
            for side in range(2):
                @pl.when(links[2 + side][0])
                def _():
                    arriving_halo(side, group).wait_recv()
            both = jnp.concatenate([halo[1, group], halo[2, group]], axis=1)
            sides = band[1:3, 0:LANES, 0:LANES].reshape(2 * LANES, LANES)
            value = partial[unit, :, inner * LANES:(inner + 1) * LANES] + dot(both, sides)
            total[group] = value.astype(BF16)
            product[group] = total[group].astype(F32)
            for row in range(ORB):
                source[group, row, 0:ORB, :] = (
                    source[group, row, 0:ORB, :] + product[group, row * ORB:(row + 1) * ORB, :]
                )
            refreshed[group] = sandwich(group)

    each(units, finish)

    for side in range(2):
        @pl.when(links[side][0])
        def _():
            for block in range(edges):
                edge_copy(side, block).wait_send()

        @pl.when(links[2 + side][0])
        def _():
            halo_sent(side).wait_send()


def finishing(rows, total, refreshed, sigma_out, g_out, sigma_near, g_near, written):
    per = LANES // rows
    square = (LANES, LANES)
    identity = jnp.where(iota(square, 0) == iota(square, 1), 1.0, 0.0).astype(BF16)
    copies = []
    for place, (values, near, out) in enumerate(((total, sigma_near, sigma_out), (refreshed, g_near, g_out))):
        for group in range(total.shape[0]):
            back = turned(identity, values[group]).astype(BF16)
            for atom in range(per):
                at = (group * per + atom) * PAIRS
                near[:, at:at + PAIRS] = back[atom * rows:(atom + 1) * rows, :]
        copies.append(pltpu.make_async_copy(near, out, written.at[place]))
        copies[-1].start()
    for copy in copies:
        copy.wait()


def compact(
    slabs, energies, rows, atoms, edge, nbrs, freqs,
    green_far, sigma_far, neighbours_far, coupling_far, down_far, up_far, offsets_far, emit_far, absorb_far,
    sigma_near, g_near,
    green, sigma_in, neighbours, coupling, send_down, send_up, offsets, w_emit, w_absorb, fetched,
    cut, across, source, product, lesser, partial, mixing, border, outgoing, arrived, crossed, halo, own_band, far_band,
    edge_send, edge_recv, cross_send, cross_recv, halo_send, halo_recv, relay_send,
):
    per = LANES // rows
    groups = atoms // per
    last = groups - 1
    half = PAIRS // 2
    middle = LANES // 2
    span = groups * LANES
    fetches = [
        pltpu.make_async_copy(far, near, fetched.at[place])
        for place, (far, near) in enumerate((
            (green_far, green), (sigma_far, sigma_in), (down_far, send_down), (up_far, send_up),
            (neighbours_far, neighbours), (coupling_far, coupling),
            (offsets_far, offsets), (emit_far, w_emit), (absorb_far, w_absorb),
        ))
    ]
    for fetch in fetches:
        fetch.start()
    my_slab = lax.axis_index("slab")
    my_energy = lax.axis_index("energy")
    ahead = 1 - 2 * (my_energy % 2)
    odd = my_slab % 2 == 1
    below, above = my_slab > 0, my_slab < slabs - 1
    receives = odd & above
    crosses = jnp.logical_not(odd) & below
    relayed = my_slab == slabs - 1
    beyond = my_energy - ahead
    inside = (beyond >= 0) & (beyond < energies)
    onward, origin = my_energy + 2 * ahead, my_energy - 2 * ahead
    relays = relayed & (onward >= 0) & (onward < energies)
    barrier = pltpu.get_barrier_semaphore()
    links = (
        (below, {"slab": my_slab - 1}),
        (above, {"slab": my_slab + 1}),
        (my_energy >= 0, {"energy": my_energy + ahead}),
        (inside, {"energy": beyond}),
    )
    greeted = links + (
        (relayed & inside, {"energy": origin}),
        (receives, {"energy": my_energy + ahead, "slab": my_slab + 1}),
        (receives & inside, {"energy": beyond, "slab": my_slab + 1}),
    )
    awaited = [there for there, _ in links] + [relays, crosses, crosses & inside]
    for there, target in greeted:
        @pl.when(there)
        def _():
            pl.semaphore_signal(barrier, inc=1, device_id=target, device_id_type=MESH)

    early = (below, above & jnp.logical_not(odd))
    for side in range(2):
        @pl.when(jnp.logical_not(early[side]))
        def _():
            arrived[side] = jnp.zeros((half, LANES), BF16)

    @pl.when(receives & jnp.logical_not(inside))
    def _():
        crossed[2] = jnp.zeros((half, LANES), BF16)

    @pl.when(jnp.logical_not(inside))
    def _():
        for group in range(groups):
            halo[2, group] = jnp.zeros((PAIRS, LANES), BF16)

    spread = (ORB * PADDED, PAIRS)
    high, low = iota(spread, 0) // PADDED, iota(spread, 0) % PADDED
    swapped = jnp.where((low < ORB) & (iota(spread, 1) == low * ORB + high), 1.0, 0.0).astype(BF16)
    compacted = (PAIRS, PAIRS)
    straight = jnp.where(iota(compacted, 0) == iota(compacted, 1), 1.0, 0.0).astype(BF16)
    square = (LANES, LANES)

    def load(slot, blocks):
        stacked = jnp.concatenate([cut[0, block] for block in blocks], axis=0)
        across[slot] = turned(swapped, stacked).reshape(ORB, PADDED, LANES)
        stacked = jnp.concatenate([cut[1, block] for block in blocks], axis=0)
        source[slot] = turned(straight, stacked)

    def sandwich(slot):
        columns = []
        for column in range(ORB):
            left = across[slot, 0] * source[slot, column:column + 1, :]
            for inner in range(1, ORB):
                at = inner * ORB + column
                left = left + across[slot, inner] * source[slot, at:at + 1, :]
            columns.append(left)
        for column in range(ORB):
            right = columns[0] * across[slot, 0, column:column + 1, :]
            for inner in range(1, ORB):
                right = right + columns[inner] * across[slot, inner, column:column + 1, :]
            product[slot, pl.ds(column, ORB, stride=ORB), :] = right[:ORB, :]
        return product[slot]

    for fetch in fetches[:4]:
        fetch.wait()
    for place, ref in enumerate((green, sigma_in)):
        for atom in range(atoms):
            cut[place, atom] = ref[:, atom * PAIRS:(atom + 1) * PAIRS]

    load(groups, [send_down[0, t] for t in range(edge)] + [send_up[0, t] for t in range(edge)])
    edges = sandwich(groups)
    top, bottom = edges[:half], edges[half:]
    lower = iota((half, LANES), 1) < middle
    outgoing[0] = jnp.where(lower, top, pltpu.roll(bottom, middle, 1)).astype(BF16)
    outgoing[1] = jnp.where(lower, pltpu.roll(top, middle, 1), bottom).astype(BF16)

    count = sum(there.astype(jnp.int32) for there in awaited)
    pl.semaphore_wait(barrier, count)

    def edge_copy(side, slot):
        return pltpu.make_async_remote_copy(
            src_ref=outgoing.at[side],
            dst_ref=arrived.at[slot],
            send_sem=edge_send.at[side],
            recv_sem=edge_recv.at[slot],
            device_id=links[side][1],
            device_id_type=MESH,
        )

    def cross_copy(kind):
        energy = (my_energy, my_energy + ahead, beyond)[kind]
        return pltpu.make_async_remote_copy(
            src_ref=outgoing.at[0],
            dst_ref=crossed.at[kind],
            send_sem=cross_send.at[kind],
            recv_sem=cross_recv.at[kind],
            device_id={"energy": energy, "slab": my_slab - 1},
            device_id_type=MESH,
        )

    def halo_copy(kind, group):
        return pltpu.make_async_remote_copy(
            src_ref=halo.at[0, group],
            dst_ref=halo.at[1 + kind, group],
            send_sem=halo_send.at[kind, group],
            recv_sem=halo_recv.at[kind, group],
            device_id=links[2 + kind][1],
            device_id_type=MESH,
        )

    def relay_copy():
        return pltpu.make_async_remote_copy(
            src_ref=halo.at[1, last],
            dst_ref=halo.at[2, last],
            send_sem=relay_send,
            recv_sem=halo_recv.at[1, last],
            device_id={"energy": onward},
            device_id_type=MESH,
        )

    sends = (odd, above)
    for side in range(2):
        @pl.when(sends[side])
        def _():
            edge_copy(side, 1 - side).start()

    for kind in range(3):
        @pl.when(crosses if kind < 2 else crosses & inside)
        def _():
            cross_copy(kind).start()

    for group in range(groups):
        load(group, range(group * per, (group + 1) * per))
    for group in range(groups):
        lesser[:, group * LANES:(group + 1) * LANES] = sandwich(group).astype(BF16)

    for fetch in fetches[4:]:
        fetch.wait()
    slots = -(-(atoms + 2 * edge) // 8) * 8
    lane_atom = iota((1, span), 1) // rows

    def lane_values(values):
        result = jnp.full((1, span), values[0])
        for place in range(1, len(values)):
            result = jnp.where(lane_atom == place, values[place], result)
        return result

    slot_of = iota((slots, span), 0)
    weights = jnp.zeros((slots, span), F32)
    for column in range(nbrs):
        atom_of = lane_values([neighbours[atom, column] for atom in range(atoms)])
        strength = lane_values([coupling[atom, column] for atom in range(atoms)])
        weights = weights + jnp.where(slot_of == atom_of, strength, 0.0)
    tall = (rows, span)
    same_energy = iota(tall, 0) == iota(tall, 1) % rows

    def expanded(at):
        return jnp.where(same_energy, jnp.broadcast_to(weights[at:at + 1, :], tall), 0.0).astype(BF16)

    for atom in range(atoms):
        mixing[atom * rows:(atom + 1) * rows, :] = expanded(atom)
    empty = jnp.zeros((middle, span), BF16)
    for side in range(2):
        start = side * LANES
        for t in range(edge):
            part = expanded(atoms + side * edge + t)
            border[start + t * rows:start + (t + 1) * rows, 0:span] = part
            border[start + middle + t * rows:start + middle + (t + 1) * rows, span:2 * span] = part
        border[start:start + middle, span:2 * span] = empty
        border[start + middle:start + LANES, 0:span] = empty

    partial[...] = dot(lesser[...], mixing[...])

    for side in range(2):
        @pl.when(early[side])
        def _():
            edge_copy(side, side).wait_recv()

    def unfolded(values):
        return jnp.concatenate([values[:, 0:span], values[:, span:2 * span]], axis=0)

    crossing = dot(jnp.concatenate([arrived[0], arrived[1]], axis=1), border[...])
    mixed = (partial[...] + unfolded(crossing)).astype(BF16)
    for group in range(groups):
        halo[0, group] = mixed[:, group * LANES:(group + 1) * LANES]

    direct = jnp.logical_not(relayed)

    @pl.when(relayed)
    def _():
        halo_copy(0, last).start()

    for group in range(groups):
        @pl.when(inside if group < last else inside & direct)
        def _():
            halo_copy(1, group).start()

        if group < last:
            halo_copy(0, group).start()

    @pl.when(direct)
    def _():
        halo_copy(0, last).start()

    same_atom = iota(square, 0) // rows == iota(square, 1) // rows
    narrow = (rows, LANES)
    distance = iota(narrow, 1) % rows - iota(narrow, 0)
    near_weight = jnp.zeros(narrow, F32)
    ahead_weight = jnp.zeros(narrow, F32)
    behind_weight = jnp.zeros(narrow, F32)
    ahead_gap = rows - ahead * distance
    behind_gap = rows + ahead * distance
    upward = ahead > 0
    for freq in range(freqs):
        offset, emit, absorb = offsets[freq], w_emit[freq], w_absorb[freq]
        near_weight = jnp.where(distance == offset, emit, near_weight)
        near_weight = jnp.where(distance == -offset, absorb, near_weight)
        ahead_weight = jnp.where(ahead_gap == offset, jnp.where(upward, absorb, emit), ahead_weight)
        behind_weight = jnp.where(behind_gap == offset, jnp.where(upward, emit, absorb), behind_weight)

    def band(weight):
        return jnp.where(same_atom, jnp.concatenate([weight] * per, axis=0), 0.0).astype(BF16)

    own_band[...] = band(near_weight)
    far_band[0:LANES, :] = band(ahead_weight)
    far_band[LANES:2 * LANES, :] = band(behind_weight)
    for group in range(groups):
        partial[:, group * LANES:(group + 1) * LANES] = dot(halo[0, group], own_band[...])

    @pl.when(relayed)
    def _():
        halo_copy(0, last).wait_recv()

    @pl.when(relays)
    def _():
        relay_copy().start()

    @pl.when(receives)
    def _():
        pieces = []
        for kind in range(3):
            if kind < 2:
                cross_copy(kind).wait_recv()
            else:
                @pl.when(inside)
                def _():
                    cross_copy(kind).wait_recv()
            pieces.append(unfolded(dot(crossed[kind], border[LANES:2 * LANES, :])).astype(BF16))
        for group in range(groups):
            lanes = slice(group * LANES, (group + 1) * LANES)
            far = jnp.concatenate([pieces[1][:, lanes], pieces[2][:, lanes]], axis=1)
            partial[:, lanes] = partial[:, lanes] + dot(pieces[0][:, lanes], own_band[...]) + dot(far, far_band[...])

    identity = jnp.where(iota(square, 0) == iota(square, 1), 1.0, 0.0).astype(BF16)

    def place_rows(near, group, values):
        back = turned(identity, values).astype(BF16)
        for atom in range(per):
            at = (group * per + atom) * PAIRS
            near[:, at:at + PAIRS] = back[atom * rows:(atom + 1) * rows, :]

    for group in range(groups):
        if group < last:
            halo_copy(0, group).wait_recv()
        else:
            @pl.when(direct)
            def _():
                halo_copy(0, last).wait_recv()

        @pl.when(inside)
        def _():
            halo_copy(1, group).wait_recv()

        both = jnp.concatenate([halo[1, group], halo[2, group]], axis=1)
        value = partial[:, group * LANES:(group + 1) * LANES] + dot(both, far_band[...])
        total = value.astype(BF16)
        place_rows(sigma_near, group, total)
        source[group] = source[group] + total.astype(F32)
        place_rows(g_near, group, sandwich(group).astype(BF16))

    for side in range(2):
        @pl.when(sends[side])
        def _():
            edge_copy(side, 1 - side).wait_send()

    for kind in range(3):
        @pl.when(crosses if kind < 2 else crosses & inside)
        def _():
            cross_copy(kind).wait_send()

    for group in range(groups):
        halo_copy(0, group).wait_send()

        @pl.when(inside if group < last else inside & direct)
        def _():
            halo_copy(1, group).wait_send()

    @pl.when(relays)
    def _():
        relay_copy().wait_send()


def delivering(sigma_near, g_near, sigma_out, g_out, written):
    copies = [
        pltpu.make_async_copy(near, out, written.at[place])
        for place, (near, out) in enumerate(((sigma_near, sigma_out), (g_near, g_out)))
    ]
    for copy in copies:
        copy.start()
    for copy in copies:
        copy.wait()


def on_device_compact(slabs, energies, green, sigma_in, *smalls):
    rows, flat = green.shape
    atoms = flat // PAIRS
    neighbours, _, send_down, _, offsets, _, _ = smalls
    edge = send_down.shape[1]
    per = LANES // rows
    groups = atoms // per
    span = groups * LANES
    vmem = pl.BlockSpec(memory_space=pltpu.VMEM)
    far = pl.BlockSpec(memory_space=pltpu.HBM)
    body = functools.partial(
        compact, slabs, energies, rows, atoms, edge, neighbours.shape[1], offsets.shape[0]
    )
    shape = jax.ShapeDtypeStruct((rows, flat), BF16)
    near_shape = pltpu.VMEM((rows, flat), BF16)
    near = pl.pallas_call(
        body,
        out_shape=(near_shape, near_shape),
        in_specs=[far] * 9,
        out_specs=(vmem, vmem),
        scratch_shapes=[
            pltpu.VMEM(green.shape, BF16),
            pltpu.VMEM(green.shape, BF16),
            *[pltpu.SMEM(small.shape, small.dtype) for small in smalls],
            pltpu.SemaphoreType.DMA((9,)),
            pltpu.VMEM((2, atoms, rows, PAIRS), BF16),
            pltpu.VMEM((groups + 1, ORB, PADDED, LANES), F32),
            pltpu.VMEM((groups + 1, PAIRS, LANES), F32),
            pltpu.VMEM((groups + 1, PAIRS, LANES), F32),
            pltpu.VMEM((PAIRS, span), BF16),
            pltpu.VMEM((PAIRS, span), F32),
            pltpu.VMEM((span, span), BF16),
            pltpu.VMEM((2 * LANES, 2 * span), BF16),
            pltpu.VMEM((2, PAIRS // 2, LANES), BF16),
            pltpu.VMEM((2, PAIRS // 2, LANES), BF16),
            pltpu.VMEM((3, PAIRS // 2, LANES), BF16),
            pltpu.VMEM((3, groups, PAIRS, LANES), BF16),
            pltpu.VMEM((LANES, LANES), BF16),
            pltpu.VMEM((2 * LANES, LANES), BF16),
            pltpu.SemaphoreType.DMA((2,)),
            pltpu.SemaphoreType.DMA((2,)),
            pltpu.SemaphoreType.DMA((3,)),
            pltpu.SemaphoreType.DMA((3,)),
            pltpu.SemaphoreType.DMA((2, groups)),
            pltpu.SemaphoreType.DMA((2, groups)),
            pltpu.SemaphoreType.DMA,
        ],
        compiler_params=pltpu.CompilerParams(
            collective_id=0, has_side_effects=True
        ),
    )(green, sigma_in, *smalls)
    return pl.pallas_call(
        delivering,
        out_shape=(shape, shape),
        in_specs=[vmem] * 2,
        out_specs=(far, far),
        scratch_shapes=[pltpu.SemaphoreType.DMA((2,))],
        compiler_params=pltpu.CompilerParams(vmem_limit_bytes=(4 + groups) << 20),
    )(*near)


def on_device(slabs, energies, green, sigma_in, neighbours, coupling, send_down, send_up, offsets, w_emit, w_absorb):
    rows, flat = green.shape
    atoms = flat // PAIRS
    edge = send_down.shape[1]
    per = LANES // rows
    groups = atoms // per
    edges = -(-edge // per)
    wide = 2 if groups % 2 == 0 else 1
    smalls = (neighbours, coupling, send_down, send_up, offsets, w_emit, w_absorb)
    if 2 * edge == per and groups == 2 and energies % 2 == 0:
        return on_device_compact(slabs, energies, green, sigma_in, *smalls)
    vmem = pl.BlockSpec(memory_space=pltpu.VMEM)
    far = pl.BlockSpec(memory_space=pltpu.HBM)
    body = functools.partial(
        kernel, slabs, energies, rows, atoms, edge, neighbours.shape[1], offsets.shape[0]
    )
    shape = jax.ShapeDtypeStruct((rows, flat), BF16)
    turned_shape = pltpu.VMEM((groups, PAIRS, LANES), BF16)
    total, refreshed = pl.pallas_call(
        body,
        out_shape=(turned_shape, turned_shape),
        in_specs=[far] * 9,
        out_specs=(vmem, vmem),
        scratch_shapes=[
            pltpu.VMEM(green.shape, BF16),
            pltpu.VMEM(green.shape, BF16),
            *[pltpu.SMEM(small.shape, small.dtype) for small in smalls],
            pltpu.SemaphoreType.DMA((9,)),
            pltpu.VMEM((groups, ORB, PADDED, LANES), F32),
            pltpu.VMEM((groups, ORB, PADDED, LANES), F32),
            pltpu.VMEM((groups, ORB, PADDED, LANES), F32),
            pltpu.VMEM((groups, PAIRS, LANES), F32),
            pltpu.VMEM((groups + 2 * edges, PAIRS, LANES), BF16),
            pltpu.VMEM((groups // wide, PAIRS, wide * LANES), F32),
            pltpu.VMEM((groups // wide, 2, groups + 2 * edges, LANES, wide * LANES), BF16),
            pltpu.VMEM((2, edges, PAIRS, LANES), BF16),
            pltpu.VMEM((3, groups, PAIRS, LANES), BF16),
            pltpu.VMEM((3, wide * LANES, wide * LANES), BF16),
            pltpu.SemaphoreType.DMA((2, edges)),
            pltpu.SemaphoreType.DMA((2, edges)),
            pltpu.SemaphoreType.DMA((2,)),
            pltpu.SemaphoreType.DMA((2, groups)),
        ],
        compiler_params=pltpu.CompilerParams(
            collective_id=0, has_side_effects=True
        ),
    )(green, sigma_in, *smalls)
    return pl.pallas_call(
        functools.partial(finishing, rows),
        out_shape=(shape, shape),
        in_specs=[vmem] * 2,
        out_specs=(far, far),
        scratch_shapes=[
            pltpu.VMEM((rows, flat), BF16),
            pltpu.VMEM((rows, flat), BF16),
            pltpu.SemaphoreType.DMA((2,)),
        ],
        compiler_params=pltpu.CompilerParams(vmem_limit_bytes=(4 + groups) << 20),
    )(total, refreshed)


def solution(mesh):
    placed = (
        P("energy", "slab"),
        P("energy", "slab"),
        P("slab", None),
        P("slab", None),
        P("slab", None),
        P("slab", None),
        P(),
        P(),
        P(),
    )
    return jax.shard_map(
        functools.partial(on_device, mesh.shape["slab"], mesh.shape["energy"]),
        mesh=mesh,
        in_specs=placed,
        out_specs=(P("energy", "slab"), P("energy", "slab")),
        check_vma=False,
    )
```

```python
import functools

import jax
import jax.numpy as jnp
from jax import lax
from jax.experimental import pallas as pl
from jax.experimental.pallas import tpu as pltpu
from jax.sharding import PartitionSpec as P

ORB = 12
PADDED = 16
PAIRS = ORB * ORB
LANES = 128
MESH = pl.DeviceIdType.MESH
F32 = jnp.float32
BF16 = jnp.bfloat16


def iota(shape, dim):
    return lax.broadcasted_iota(jnp.int32, shape, dim)


def turned(matrix, block):
    return lax.dot_general(matrix, block, (((1,), (1,)), ((), ())), preferred_element_type=F32)


def dot(left, right):
    return jnp.dot(left, right, preferred_element_type=F32)


def each(count, body):
    if count <= 2:
        for index in range(count):
            body(index)
    else:
        lax.fori_loop(0, count, lambda index, carry: (body(index), carry)[1], 0)


def kernel(
    slabs, energies, rows, atoms, edge, nbrs, freqs,
    green_far, sigma_far, neighbours_far, coupling_far, down_far, up_far, offsets_far, emit_far, absorb_far,
    total, refreshed,
    green, sigma_in, neighbours, coupling, send_down, send_up, offsets, w_emit, w_absorb, fetched,
    plain, across, source, product, lesser, partial, mixing, outgoing, halo, band,
    edge_send, edge_recv, halo_send, halo_recv,
):
    per = LANES // rows
    groups = atoms // per
    edges = outgoing.shape[1]
    fetches = [
        pltpu.make_async_copy(far, near, fetched.at[place])
        for place, (far, near) in enumerate((
            (green_far, green), (sigma_far, sigma_in), (down_far, send_down), (up_far, send_up),
            (neighbours_far, neighbours), (coupling_far, coupling),
            (offsets_far, offsets), (emit_far, w_emit), (absorb_far, w_absorb),
        ))
    ]
    for fetch in fetches:
        fetch.start()
    my_slab = lax.axis_index("slab")
    my_energy = lax.axis_index("energy")
    barrier = pltpu.get_barrier_semaphore()
    links = (
        (my_slab > 0, {"slab": my_slab - 1}),
        (my_slab < slabs - 1, {"slab": my_slab + 1}),
        (my_energy > 0, {"energy": my_energy - 1}),
        (my_energy < energies - 1, {"energy": my_energy + 1}),
    )
    for there, target in links:
        @pl.when(there)
        def _():
            pl.semaphore_signal(barrier, inc=1, device_id=target, device_id_type=MESH)

    for side in range(2):
        @pl.when(jnp.logical_not(links[side][0]))
        def _():
            for block in range(edges):
                lesser[groups + side * edges + block] = jnp.zeros((PAIRS, LANES), BF16)

        @pl.when(jnp.logical_not(links[2 + side][0]))
        def _():
            for block in range(groups):
                halo[1 + side, block] = jnp.zeros((PAIRS, LANES), BF16)

    spread = (ORB * PADDED, PAIRS)
    high, low = iota(spread, 0) // PADDED, iota(spread, 0) % PADDED
    real = low < ORB
    straight = jnp.where(real & (iota(spread, 1) == high * ORB + low), 1.0, 0.0).astype(BF16)
    swapped = jnp.where(real & (iota(spread, 1) == low * ORB + high), 1.0, 0.0).astype(BF16)
    square = (LANES, LANES)
    same_energy = iota(square, 0) % rows == iota(square, 1) % rows
    lane_atom = iota((1, LANES), 1) // rows

    fetches[0].wait()
    fetches[1].wait()

    def gathered(ref, group):
        pieces = [
            ref[:, (group * per + atom) * PAIRS:(group * per + atom + 1) * PAIRS]
            for atom in range(per)
        ]
        return jnp.concatenate(pieces, axis=0)

    for group in range(groups):
        stacked = gathered(green, group)
        plain[group] = turned(straight, stacked).reshape(ORB, PADDED, LANES)
        across[group] = turned(swapped, stacked).reshape(ORB, PADDED, LANES)
        source[group] = turned(straight, gathered(sigma_in, group)).reshape(ORB, PADDED, LANES)

    def sandwich(group):
        for row in range(ORB):
            left = plain[group, row, 0:1, :] * source[group, 0]
            for inner in range(1, ORB):
                left = left + plain[group, row, inner:inner + 1, :] * source[group, inner]
            right = left[0:1, :] * across[group, 0]
            for inner in range(1, ORB):
                right = right + left[inner:inner + 1, :] * across[group, inner]
            product[group, row * ORB:(row + 1) * ORB, :] = right[:ORB, :]
        return product[group].astype(BF16)

    def first(group):
        lesser[group] = sandwich(group)

    each(groups, first)
    for fetch in fetches[2:]:
        fetch.wait()

    def lane_values(values):
        result = jnp.full((1, LANES), values[0])
        for place in range(1, len(values)):
            result = jnp.where(lane_atom == place, values[place], result)
        return result

    def expand(pieces):
        full = jnp.concatenate([jnp.broadcast_to(piece, (rows, LANES)) for piece in pieces], axis=0)
        return jnp.where(same_energy, full, 0.0).astype(BF16)

    for side, sent in ((0, send_down), (1, send_up)):
        for block in range(edges):
            first_slot = block * per
            wanted = lane_values(
                [sent[0, first_slot + t] if first_slot + t < edge else jnp.int32(-1) for t in range(per)]
            )
            chosen = jnp.zeros((PAIRS, LANES), F32)
            for group in range(groups):
                pieces = [
                    jnp.where(wanted == group * per + atom, 1.0, 0.0) for atom in range(per)
                ]
                chosen = chosen + dot(lesser[group], expand(pieces))
            outgoing[side, block] = chosen.astype(BF16)

    count = sum(there.astype(jnp.int32) for there, _ in links)
    pl.semaphore_wait(barrier, count)

    def edge_copy(side, block):
        return pltpu.make_async_remote_copy(
            src_ref=outgoing.at[side, block],
            dst_ref=lesser.at[groups + (1 - side) * edges + block],
            send_sem=edge_send.at[side, block],
            recv_sem=edge_recv.at[1 - side, block],
            device_id=links[side][1],
            device_id_type=MESH,
        )

    def arriving_edge(side, block):
        return pltpu.make_async_remote_copy(
            src_ref=outgoing.at[side, block],
            dst_ref=lesser.at[groups + side * edges + block],
            send_sem=edge_send.at[side, block],
            recv_sem=edge_recv.at[side, block],
            device_id=links[side][1],
            device_id_type=MESH,
        )

    def halo_copy(side, group):
        return pltpu.make_async_remote_copy(
            src_ref=halo.at[0, group],
            dst_ref=halo.at[2 - side, group],
            send_sem=halo_send.at[side],
            recv_sem=halo_recv.at[1 - side, group],
            device_id=links[2 + side][1],
            device_id_type=MESH,
        )

    def halo_sent(side):
        return pltpu.make_async_remote_copy(
            src_ref=halo.at[0],
            dst_ref=halo.at[2 - side],
            send_sem=halo_send.at[side],
            recv_sem=halo_recv.at[1 - side, 0],
            device_id=links[2 + side][1],
            device_id_type=MESH,
        )

    def arriving_halo(side, group):
        return pltpu.make_async_remote_copy(
            src_ref=halo.at[0, group],
            dst_ref=halo.at[1 + side, group],
            send_sem=halo_send.at[side],
            recv_sem=halo_recv.at[side, group],
            device_id=links[2 + side][1],
            device_id_type=MESH,
        )

    for side in range(2):
        @pl.when(links[side][0])
        def _():
            for block in range(edges):
                edge_copy(side, block).start()

    slots = -(-(atoms + 2 * edge) // 8) * 8
    blocks = groups + 2 * edges
    wide = 2 if groups % 2 == 0 else 1
    units = groups // wide

    def weigh(unit):
        for inner in range(wide):
            group = unit * wide + inner
            lanes = slice(inner * LANES, (inner + 1) * LANES)
            slot = iota((slots, LANES), 0)
            weights = jnp.zeros((slots, LANES), F32)
            for column in range(nbrs):
                atom_of = lane_values([neighbours[group * per + t, column] for t in range(per)])
                strength = lane_values([coupling[group * per + t, column] for t in range(per)])
                weights = weights + jnp.where(slot == atom_of, strength, 0.0)
            coarse = weights.astype(BF16).astype(F32)
            for level, part in enumerate((coarse, weights - coarse)):
                for block in range(blocks):
                    side = (block - groups) // edges
                    pieces = []
                    for t in range(per):
                        number = block * per + t if block < groups else ((block - groups) % edges) * per + t
                        at = number if block < groups else atoms + side * edge + number
                        known = block < groups or number < edge
                        pieces.append(part[at:at + 1, :] if known else jnp.zeros((1, LANES), F32))
                    mixing[unit, level, block, :, lanes] = expand(pieces)

    each(units, weigh)

    def joined(unit, first, last):
        value = None
        for start in range(first, last, 2):
            stop = min(start + 2, last)
            left = jnp.concatenate([lesser[block] for block in range(start, stop)], axis=1)
            for level in range(2):
                right = mixing[unit, level, start:stop].reshape((stop - start) * LANES, wide * LANES)
                term = dot(left, right)
                value = term if value is None else value + term
        return value

    def mix_own(unit):
        partial[unit] = joined(unit, 0, groups)

    each(units, mix_own)

    for side in range(2):
        @pl.when(links[side][0])
        def _():
            for block in range(edges):
                arriving_edge(side, block).wait_recv()

    def mix_border(unit):
        value = (partial[unit] + joined(unit, groups, blocks)).astype(BF16)
        for inner in range(wide):
            group = unit * wide + inner
            halo[0, group] = value[:, inner * LANES:(inner + 1) * LANES]
            for side in range(2):
                @pl.when(links[2 + side][0])
                def _():
                    halo_copy(side, group).start()

    each(units, mix_border)

    tall = (rows, LANES)
    same_atom = iota(square, 0) // rows == iota(square, 1) // rows
    for place, shift in enumerate((0, rows, -rows)):
        distance = iota(tall, 1) % rows - iota(tall, 0) + shift
        weight = jnp.zeros(tall, F32)
        for freq in range(freqs):
            weight = jnp.where(distance == offsets[freq], w_emit[freq], weight)
            weight = jnp.where(distance == -offsets[freq], w_absorb[freq], weight)
        full = jnp.concatenate([weight] * per, axis=0)
        full = jnp.where(same_atom, full, 0.0).astype(BF16)
        for inner in range(wide):
            for other in range(wide):
                band[place, inner * LANES:(inner + 1) * LANES, other * LANES:(other + 1) * LANES] = (
                    full if inner == other else jnp.zeros(square, BF16)
                )

    def neighbour(place, unit):
        return [halo[place, unit * wide + inner] for inner in range(wide)]

    def band_own(unit):
        partial[unit] = dot(jnp.concatenate(neighbour(0, unit), axis=1), band[0])

    each(units, band_own)

    def finish(unit):
        for inner in range(wide):
            group = unit * wide + inner
            for side in range(2):
                @pl.when(links[2 + side][0])
                def _():
                    arriving_halo(side, group).wait_recv()
            both = jnp.concatenate([halo[1, group], halo[2, group]], axis=1)
            sides = band[1:3, 0:LANES, 0:LANES].reshape(2 * LANES, LANES)
            value = partial[unit, :, inner * LANES:(inner + 1) * LANES] + dot(both, sides)
            total[group] = value.astype(BF16)
            product[group] = total[group].astype(F32)
            for row in range(ORB):
                source[group, row, 0:ORB, :] = (
                    source[group, row, 0:ORB, :] + product[group, row * ORB:(row + 1) * ORB, :]
                )
            refreshed[group] = sandwich(group)

    each(units, finish)

    for side in range(2):
        @pl.when(links[side][0])
        def _():
            for block in range(edges):
                edge_copy(side, block).wait_send()

        @pl.when(links[2 + side][0])
        def _():
            halo_sent(side).wait_send()


def finishing(rows, total, refreshed, sigma_out, g_out, sigma_near, g_near, written):
    per = LANES // rows
    square = (LANES, LANES)
    identity = jnp.where(iota(square, 0) == iota(square, 1), 1.0, 0.0).astype(BF16)
    copies = []
    for place, (values, near, out) in enumerate(((total, sigma_near, sigma_out), (refreshed, g_near, g_out))):
        for group in range(total.shape[0]):
            back = turned(identity, values[group]).astype(BF16)
            for atom in range(per):
                at = (group * per + atom) * PAIRS
                near[:, at:at + PAIRS] = back[atom * rows:(atom + 1) * rows, :]
        copies.append(pltpu.make_async_copy(near, out, written.at[place]))
        copies[-1].start()
    for copy in copies:
        copy.wait()


def compact(
    slabs, energies, rows, atoms, edge, nbrs, freqs,
    green_far, sigma_far, neighbours_far, coupling_far, down_far, up_far, offsets_far, emit_far, absorb_far,
    sigma_near, g_near,
    green, sigma_in, neighbours, coupling, send_down, send_up, offsets, w_emit, w_absorb, fetched,
    cut, across, source, product, lesser, partial, mixing, border, outgoing, arrived, halo, own_band, far_band,
    edge_send, edge_recv, halo_send, halo_recv, relay_send,
):
    per = LANES // rows
    groups = atoms // per
    last = groups - 1
    half = PAIRS // 2
    middle = LANES // 2
    span = groups * LANES
    fetches = [
        pltpu.make_async_copy(far, near, fetched.at[place])
        for place, (far, near) in enumerate((
            (green_far, green), (sigma_far, sigma_in), (down_far, send_down), (up_far, send_up),
            (neighbours_far, neighbours), (coupling_far, coupling),
            (offsets_far, offsets), (emit_far, w_emit), (absorb_far, w_absorb),
        ))
    ]
    for fetch in fetches:
        fetch.start()
    my_slab = lax.axis_index("slab")
    my_energy = lax.axis_index("energy")
    ahead = 1 - 2 * (my_energy % 2)
    odd = my_slab % 2 == 1
    even = jnp.logical_not(odd)
    exists = (my_slab > 0, my_slab < slabs - 1)
    relayed = my_slab == slabs - 1
    beyond = my_energy - ahead
    inside = (beyond >= 0) & (beyond < energies)
    onward, origin = my_energy + 2 * ahead, my_energy - 2 * ahead
    relays = relayed & (onward >= 0) & (onward < energies)
    barrier = pltpu.get_barrier_semaphore()
    links = (
        (exists[0], {"slab": my_slab - 1}),
        (exists[1], {"slab": my_slab + 1}),
        (my_energy >= 0, {"energy": my_energy + ahead}),
        (inside, {"energy": beyond}),
    )
    greeted = list(links) + [(relayed & inside, {"energy": origin})]
    awaited = [there for there, _ in links] + [relays]
    for side in range(2):
        for energy, there in ((my_energy + ahead, exists[side]), (beyond, exists[side] & inside)):
            greeted.append((odd & there, {"energy": energy, "slab": my_slab + 2 * side - 1}))
            awaited.append(even & there)
    for there, target in greeted:
        @pl.when(there)
        def _():
            pl.semaphore_signal(barrier, inc=1, device_id=target, device_id_type=MESH)

    nothing = jnp.zeros((half, LANES), BF16)
    for side in range(2):
        @pl.when(jnp.logical_not(exists[side]))
        def _():
            for kind in range(3):
                arrived[side, kind] = nothing

    @pl.when(jnp.logical_not(inside))
    def _():
        for side in range(2):
            arrived[side, 2] = nothing
        for group in range(groups):
            halo[2, group] = jnp.zeros((PAIRS, LANES), BF16)

    spread = (ORB * PADDED, PAIRS)
    high, low = iota(spread, 0) // PADDED, iota(spread, 0) % PADDED
    swapped = jnp.where((low < ORB) & (iota(spread, 1) == low * ORB + high), 1.0, 0.0).astype(BF16)
    compacted = (PAIRS, PAIRS)
    straight = jnp.where(iota(compacted, 0) == iota(compacted, 1), 1.0, 0.0).astype(BF16)
    square = (LANES, LANES)

    def load(slot, blocks):
        stacked = jnp.concatenate([cut[0, block] for block in blocks], axis=0)
        across[slot] = turned(swapped, stacked).reshape(ORB, PADDED, LANES)
        stacked = jnp.concatenate([cut[1, block] for block in blocks], axis=0)
        source[slot] = turned(straight, stacked)

    def sandwich(slot):
        columns = []
        for column in range(ORB):
            left = across[slot, 0] * source[slot, column:column + 1, :]
            for inner in range(1, ORB):
                at = inner * ORB + column
                left = left + across[slot, inner] * source[slot, at:at + 1, :]
            columns.append(left)
        for column in range(ORB):
            right = columns[0] * across[slot, 0, column:column + 1, :]
            for inner in range(1, ORB):
                right = right + columns[inner] * across[slot, inner, column:column + 1, :]
            product[slot, pl.ds(column, ORB, stride=ORB), :] = right[:ORB, :]
        return product[slot]

    for fetch in fetches[:4]:
        fetch.wait()
    for place, ref in enumerate((green, sigma_in)):
        for atom in range(atoms):
            cut[place, atom] = ref[:, atom * PAIRS:(atom + 1) * PAIRS]

    load(groups, [send_down[0, t] for t in range(edge)] + [send_up[0, t] for t in range(edge)])
    edges = sandwich(groups)
    top, bottom = edges[:half], edges[half:]
    lower = iota((half, LANES), 1) < middle
    outgoing[0] = jnp.where(lower, top, pltpu.roll(bottom, middle, 1)).astype(BF16)
    outgoing[1] = jnp.where(lower, pltpu.roll(top, middle, 1), bottom).astype(BF16)

    count = sum(there.astype(jnp.int32) for there in awaited)
    pl.semaphore_wait(barrier, count)

    def edge_copy(side, kind, slot):
        energy = (my_energy, my_energy + ahead, beyond)[kind]
        return pltpu.make_async_remote_copy(
            src_ref=outgoing.at[side],
            dst_ref=arrived.at[slot, kind],
            send_sem=edge_send.at[side, kind],
            recv_sem=edge_recv.at[slot, kind],
            device_id={"energy": energy, "slab": my_slab + 2 * side - 1},
            device_id_type=MESH,
        )

    def taking(side, kind, role):
        there = exists[side] if kind == 0 else exists[side] & role
        return there if kind < 2 else there & inside

    def awaiting(kinds, role):
        for kind in kinds:
            for side in range(2):
                @pl.when(taking(side, kind, role))
                def _():
                    edge_copy(side, kind, side).wait_recv()

    def halo_copy(kind, group):
        return pltpu.make_async_remote_copy(
            src_ref=halo.at[0, group],
            dst_ref=halo.at[1 + kind, group],
            send_sem=halo_send.at[kind, group],
            recv_sem=halo_recv.at[kind, group],
            device_id=links[2 + kind][1],
            device_id_type=MESH,
        )

    def relay_copy():
        return pltpu.make_async_remote_copy(
            src_ref=halo.at[1, last],
            dst_ref=halo.at[2, last],
            send_sem=relay_send,
            recv_sem=halo_recv.at[1, last],
            device_id={"energy": onward},
            device_id_type=MESH,
        )

    for kind in (2, 1, 0):
        for side in range(2):
            @pl.when(taking(side, kind, even))
            def _():
                edge_copy(side, kind, 1 - side).start()

    for group in range(groups):
        load(group, range(group * per, (group + 1) * per))
    for group in range(groups):
        lesser[:, group * LANES:(group + 1) * LANES] = sandwich(group).astype(BF16)

    for fetch in fetches[4:]:
        fetch.wait()
    slots = -(-(atoms + 2 * edge) // 8) * 8
    lane_atom = iota((1, span), 1) // rows

    def lane_values(values):
        result = jnp.full((1, span), values[0])
        for place in range(1, len(values)):
            result = jnp.where(lane_atom == place, values[place], result)
        return result

    slot_of = iota((slots, span), 0)
    weights = jnp.zeros((slots, span), F32)
    for column in range(nbrs):
        atom_of = lane_values([neighbours[atom, column] for atom in range(atoms)])
        strength = lane_values([coupling[atom, column] for atom in range(atoms)])
        weights = weights + jnp.where(slot_of == atom_of, strength, 0.0)
    tall = (rows, span)
    same_energy = iota(tall, 0) == iota(tall, 1) % rows

    def expanded(at):
        return jnp.where(same_energy, jnp.broadcast_to(weights[at:at + 1, :], tall), 0.0).astype(BF16)

    for atom in range(atoms):
        mixing[atom * rows:(atom + 1) * rows, :] = expanded(atom)
    empty = jnp.zeros((middle, span), BF16)
    for side in range(2):
        start = side * LANES
        for t in range(edge):
            part = expanded(atoms + side * edge + t)
            border[start + t * rows:start + (t + 1) * rows, 0:span] = part
            border[start + middle + t * rows:start + middle + (t + 1) * rows, span:2 * span] = part
        border[start:start + middle, span:2 * span] = empty
        border[start + middle:start + LANES, 0:span] = empty

    partial[...] = dot(lesser[...], mixing[...])

    def crossing(kind):
        value = dot(jnp.concatenate([arrived[0, kind], arrived[1, kind]], axis=1), border[...])
        return jnp.concatenate([value[:, 0:span], value[:, span:2 * span]], axis=0)

    def settle(mixed):
        for group in range(groups):
            halo[0, group] = mixed[:, group * LANES:(group + 1) * LANES].astype(BF16)

    @pl.when(even)
    def _():
        awaiting((0,), odd)
        settle(partial[...] + crossing(0))

    @pl.when(odd)
    def _():
        settle(partial[...])

    direct = jnp.logical_not(relayed)

    @pl.when(relayed)
    def _():
        halo_copy(0, last).start()

    for group in range(groups):
        @pl.when(inside if group < last else inside & direct)
        def _():
            halo_copy(1, group).start()

        if group < last:
            halo_copy(0, group).start()

    @pl.when(direct)
    def _():
        halo_copy(0, last).start()

    same_atom = iota(square, 0) // rows == iota(square, 1) // rows
    narrow = (rows, LANES)
    distance = iota(narrow, 1) % rows - iota(narrow, 0)
    near_weight = jnp.zeros(narrow, F32)
    ahead_weight = jnp.zeros(narrow, F32)
    behind_weight = jnp.zeros(narrow, F32)
    ahead_gap = rows - ahead * distance
    behind_gap = rows + ahead * distance
    upward = ahead > 0
    for freq in range(freqs):
        offset, emit, absorb = offsets[freq], w_emit[freq], w_absorb[freq]
        near_weight = jnp.where(distance == offset, emit, near_weight)
        near_weight = jnp.where(distance == -offset, absorb, near_weight)
        ahead_weight = jnp.where(ahead_gap == offset, jnp.where(upward, absorb, emit), ahead_weight)
        behind_weight = jnp.where(behind_gap == offset, jnp.where(upward, emit, absorb), behind_weight)

    def band(weight):
        return jnp.where(same_atom, jnp.concatenate([weight] * per, axis=0), 0.0).astype(BF16)

    own_band[...] = band(near_weight)
    far_band[0:LANES, :] = band(ahead_weight)
    far_band[LANES:2 * LANES, :] = band(behind_weight)
    for group in range(groups):
        partial[:, group * LANES:(group + 1) * LANES] = dot(halo[0, group], own_band[...])

    @pl.when(relayed)
    def _():
        halo_copy(0, last).wait_recv()

    @pl.when(relays)
    def _():
        relay_copy().start()

    @pl.when(odd)
    def _():
        awaiting((0, 1, 2), odd)
        pieces = [crossing(kind).astype(BF16) for kind in range(3)]
        for group in range(groups):
            lanes = slice(group * LANES, (group + 1) * LANES)
            far = jnp.concatenate([pieces[1][:, lanes], pieces[2][:, lanes]], axis=1)
            partial[:, lanes] = partial[:, lanes] + dot(pieces[0][:, lanes], own_band[...]) + dot(far, far_band[...])

    identity = jnp.where(iota(square, 0) == iota(square, 1), 1.0, 0.0).astype(BF16)

    def place_rows(near, group, values):
        back = turned(identity, values).astype(BF16)
        for atom in range(per):
            at = (group * per + atom) * PAIRS
            near[:, at:at + PAIRS] = back[atom * rows:(atom + 1) * rows, :]

    for group in range(groups):
        if group < last:
            halo_copy(0, group).wait_recv()
        else:
            @pl.when(direct)
            def _():
                halo_copy(0, last).wait_recv()

        @pl.when(inside)
        def _():
            halo_copy(1, group).wait_recv()

        both = jnp.concatenate([halo[1, group], halo[2, group]], axis=1)
        value = partial[:, group * LANES:(group + 1) * LANES] + dot(both, far_band[...])
        total = value.astype(BF16)
        place_rows(sigma_near, group, total)
        source[group] = source[group] + total.astype(F32)
        place_rows(g_near, group, sandwich(group).astype(BF16))

    for kind in range(3):
        for side in range(2):
            @pl.when(taking(side, kind, even))
            def _():
                edge_copy(side, kind, 1 - side).wait_send()

    for group in range(groups):
        halo_copy(0, group).wait_send()

        @pl.when(inside if group < last else inside & direct)
        def _():
            halo_copy(1, group).wait_send()

    @pl.when(relays)
    def _():
        relay_copy().wait_send()


def delivering(sigma_near, g_near, sigma_out, g_out, written):
    copies = [
        pltpu.make_async_copy(near, out, written.at[place])
        for place, (near, out) in enumerate(((sigma_near, sigma_out), (g_near, g_out)))
    ]
    for copy in copies:
        copy.start()
    for copy in copies:
        copy.wait()


def on_device_compact(slabs, energies, green, sigma_in, *smalls):
    rows, flat = green.shape
    atoms = flat // PAIRS
    neighbours, _, send_down, _, offsets, _, _ = smalls
    edge = send_down.shape[1]
    per = LANES // rows
    groups = atoms // per
    span = groups * LANES
    vmem = pl.BlockSpec(memory_space=pltpu.VMEM)
    far = pl.BlockSpec(memory_space=pltpu.HBM)
    body = functools.partial(
        compact, slabs, energies, rows, atoms, edge, neighbours.shape[1], offsets.shape[0]
    )
    shape = jax.ShapeDtypeStruct((rows, flat), BF16)
    near_shape = pltpu.VMEM((rows, flat), BF16)
    near = pl.pallas_call(
        body,
        out_shape=(near_shape, near_shape),
        in_specs=[far] * 9,
        out_specs=(vmem, vmem),
        scratch_shapes=[
            pltpu.VMEM(green.shape, BF16),
            pltpu.VMEM(green.shape, BF16),
            *[pltpu.SMEM(small.shape, small.dtype) for small in smalls],
            pltpu.SemaphoreType.DMA((9,)),
            pltpu.VMEM((2, atoms, rows, PAIRS), BF16),
            pltpu.VMEM((groups + 1, ORB, PADDED, LANES), F32),
            pltpu.VMEM((groups + 1, PAIRS, LANES), F32),
            pltpu.VMEM((groups + 1, PAIRS, LANES), F32),
            pltpu.VMEM((PAIRS, span), BF16),
            pltpu.VMEM((PAIRS, span), F32),
            pltpu.VMEM((span, span), BF16),
            pltpu.VMEM((2 * LANES, 2 * span), BF16),
            pltpu.VMEM((2, PAIRS // 2, LANES), BF16),
            pltpu.VMEM((2, 3, PAIRS // 2, LANES), BF16),
            pltpu.VMEM((3, groups, PAIRS, LANES), BF16),
            pltpu.VMEM((LANES, LANES), BF16),
            pltpu.VMEM((2 * LANES, LANES), BF16),
            pltpu.SemaphoreType.DMA((2, 3)),
            pltpu.SemaphoreType.DMA((2, 3)),
            pltpu.SemaphoreType.DMA((2, groups)),
            pltpu.SemaphoreType.DMA((2, groups)),
            pltpu.SemaphoreType.DMA,
        ],
        compiler_params=pltpu.CompilerParams(
            collective_id=0, has_side_effects=True
        ),
    )(green, sigma_in, *smalls)
    return pl.pallas_call(
        delivering,
        out_shape=(shape, shape),
        in_specs=[vmem] * 2,
        out_specs=(far, far),
        scratch_shapes=[pltpu.SemaphoreType.DMA((2,))],
        compiler_params=pltpu.CompilerParams(vmem_limit_bytes=(4 + groups) << 20),
    )(*near)


def on_device(slabs, energies, green, sigma_in, neighbours, coupling, send_down, send_up, offsets, w_emit, w_absorb):
    rows, flat = green.shape
    atoms = flat // PAIRS
    edge = send_down.shape[1]
    per = LANES // rows
    groups = atoms // per
    edges = -(-edge // per)
    wide = 2 if groups % 2 == 0 else 1
    smalls = (neighbours, coupling, send_down, send_up, offsets, w_emit, w_absorb)
    if 2 * edge == per and groups == 2 and energies % 2 == 0:
        return on_device_compact(slabs, energies, green, sigma_in, *smalls)
    vmem = pl.BlockSpec(memory_space=pltpu.VMEM)
    far = pl.BlockSpec(memory_space=pltpu.HBM)
    body = functools.partial(
        kernel, slabs, energies, rows, atoms, edge, neighbours.shape[1], offsets.shape[0]
    )
    shape = jax.ShapeDtypeStruct((rows, flat), BF16)
    turned_shape = pltpu.VMEM((groups, PAIRS, LANES), BF16)
    total, refreshed = pl.pallas_call(
        body,
        out_shape=(turned_shape, turned_shape),
        in_specs=[far] * 9,
        out_specs=(vmem, vmem),
        scratch_shapes=[
            pltpu.VMEM(green.shape, BF16),
            pltpu.VMEM(green.shape, BF16),
            *[pltpu.SMEM(small.shape, small.dtype) for small in smalls],
            pltpu.SemaphoreType.DMA((9,)),
            pltpu.VMEM((groups, ORB, PADDED, LANES), F32),
            pltpu.VMEM((groups, ORB, PADDED, LANES), F32),
            pltpu.VMEM((groups, ORB, PADDED, LANES), F32),
            pltpu.VMEM((groups, PAIRS, LANES), F32),
            pltpu.VMEM((groups + 2 * edges, PAIRS, LANES), BF16),
            pltpu.VMEM((groups // wide, PAIRS, wide * LANES), F32),
            pltpu.VMEM((groups // wide, 2, groups + 2 * edges, LANES, wide * LANES), BF16),
            pltpu.VMEM((2, edges, PAIRS, LANES), BF16),
            pltpu.VMEM((3, groups, PAIRS, LANES), BF16),
            pltpu.VMEM((3, wide * LANES, wide * LANES), BF16),
            pltpu.SemaphoreType.DMA((2, edges)),
            pltpu.SemaphoreType.DMA((2, edges)),
            pltpu.SemaphoreType.DMA((2,)),
            pltpu.SemaphoreType.DMA((2, groups)),
        ],
        compiler_params=pltpu.CompilerParams(
            collective_id=0, has_side_effects=True
        ),
    )(green, sigma_in, *smalls)
    return pl.pallas_call(
        functools.partial(finishing, rows),
        out_shape=(shape, shape),
        in_specs=[vmem] * 2,
        out_specs=(far, far),
        scratch_shapes=[
            pltpu.VMEM((rows, flat), BF16),
            pltpu.VMEM((rows, flat), BF16),
            pltpu.SemaphoreType.DMA((2,)),
        ],
        compiler_params=pltpu.CompilerParams(vmem_limit_bytes=(4 + groups) << 20),
    )(total, refreshed)


def solution(mesh):
    placed = (
        P("energy", "slab"),
        P("energy", "slab"),
        P("slab", None),
        P("slab", None),
        P("slab", None),
        P("slab", None),
        P(),
        P(),
        P(),
    )
    return jax.shard_map(
        functools.partial(on_device, mesh.shape["slab"], mesh.shape["energy"]),
        mesh=mesh,
        in_specs=placed,
        out_specs=(P("energy", "slab"), P("energy", "slab")),
        check_vma=False,
    )
```

```python
import functools

import jax
import jax.numpy as jnp
from jax import lax
from jax.experimental import pallas as pl
from jax.experimental.pallas import tpu as pltpu
from jax.sharding import PartitionSpec as P

ORB = 12
PADDED = 16
PAIRS = ORB * ORB
LANES = 128
MESH = pl.DeviceIdType.MESH
F32 = jnp.float32
BF16 = jnp.bfloat16


def iota(shape, dim):
    return lax.broadcasted_iota(jnp.int32, shape, dim)


def turned(matrix, block):
    return lax.dot_general(matrix, block, (((1,), (1,)), ((), ())), preferred_element_type=F32)


def dot(left, right):
    return jnp.dot(left, right, preferred_element_type=F32)


def each(count, body):
    if count <= 2:
        for index in range(count):
            body(index)
    else:
        lax.fori_loop(0, count, lambda index, carry: (body(index), carry)[1], 0)


def kernel(
    slabs, energies, rows, atoms, edge, nbrs, freqs,
    green_far, sigma_far, neighbours_far, coupling_far, down_far, up_far, offsets_far, emit_far, absorb_far,
    total, refreshed,
    green, sigma_in, neighbours, coupling, send_down, send_up, offsets, w_emit, w_absorb, fetched,
    plain, across, source, product, lesser, partial, mixing, outgoing, halo, band,
    edge_send, edge_recv, halo_send, halo_recv,
):
    per = LANES // rows
    groups = atoms // per
    edges = outgoing.shape[1]
    fetches = [
        pltpu.make_async_copy(far, near, fetched.at[place])
        for place, (far, near) in enumerate((
            (green_far, green), (sigma_far, sigma_in), (down_far, send_down), (up_far, send_up),
            (neighbours_far, neighbours), (coupling_far, coupling),
            (offsets_far, offsets), (emit_far, w_emit), (absorb_far, w_absorb),
        ))
    ]
    for fetch in fetches:
        fetch.start()
    my_slab = lax.axis_index("slab")
    my_energy = lax.axis_index("energy")
    barrier = pltpu.get_barrier_semaphore()
    links = (
        (my_slab > 0, {"slab": my_slab - 1}),
        (my_slab < slabs - 1, {"slab": my_slab + 1}),
        (my_energy > 0, {"energy": my_energy - 1}),
        (my_energy < energies - 1, {"energy": my_energy + 1}),
    )
    for there, target in links:
        @pl.when(there)
        def _():
            pl.semaphore_signal(barrier, inc=1, device_id=target, device_id_type=MESH)

    for side in range(2):
        @pl.when(jnp.logical_not(links[side][0]))
        def _():
            for block in range(edges):
                lesser[groups + side * edges + block] = jnp.zeros((PAIRS, LANES), BF16)

        @pl.when(jnp.logical_not(links[2 + side][0]))
        def _():
            for block in range(groups):
                halo[1 + side, block] = jnp.zeros((PAIRS, LANES), BF16)

    spread = (ORB * PADDED, PAIRS)
    high, low = iota(spread, 0) // PADDED, iota(spread, 0) % PADDED
    real = low < ORB
    straight = jnp.where(real & (iota(spread, 1) == high * ORB + low), 1.0, 0.0).astype(BF16)
    swapped = jnp.where(real & (iota(spread, 1) == low * ORB + high), 1.0, 0.0).astype(BF16)
    square = (LANES, LANES)
    same_energy = iota(square, 0) % rows == iota(square, 1) % rows
    lane_atom = iota((1, LANES), 1) // rows

    fetches[0].wait()
    fetches[1].wait()

    def gathered(ref, group):
        pieces = [
            ref[:, (group * per + atom) * PAIRS:(group * per + atom + 1) * PAIRS]
            for atom in range(per)
        ]
        return jnp.concatenate(pieces, axis=0)

    for group in range(groups):
        stacked = gathered(green, group)
        plain[group] = turned(straight, stacked).reshape(ORB, PADDED, LANES)
        across[group] = turned(swapped, stacked).reshape(ORB, PADDED, LANES)
        source[group] = turned(straight, gathered(sigma_in, group)).reshape(ORB, PADDED, LANES)

    def sandwich(group):
        for row in range(ORB):
            left = plain[group, row, 0:1, :] * source[group, 0]
            for inner in range(1, ORB):
                left = left + plain[group, row, inner:inner + 1, :] * source[group, inner]
            right = left[0:1, :] * across[group, 0]
            for inner in range(1, ORB):
                right = right + left[inner:inner + 1, :] * across[group, inner]
            product[group, row * ORB:(row + 1) * ORB, :] = right[:ORB, :]
        return product[group].astype(BF16)

    def first(group):
        lesser[group] = sandwich(group)

    each(groups, first)
    for fetch in fetches[2:]:
        fetch.wait()

    def lane_values(values):
        result = jnp.full((1, LANES), values[0])
        for place in range(1, len(values)):
            result = jnp.where(lane_atom == place, values[place], result)
        return result

    def expand(pieces):
        full = jnp.concatenate([jnp.broadcast_to(piece, (rows, LANES)) for piece in pieces], axis=0)
        return jnp.where(same_energy, full, 0.0).astype(BF16)

    for side, sent in ((0, send_down), (1, send_up)):
        for block in range(edges):
            first_slot = block * per
            wanted = lane_values(
                [sent[0, first_slot + t] if first_slot + t < edge else jnp.int32(-1) for t in range(per)]
            )
            chosen = jnp.zeros((PAIRS, LANES), F32)
            for group in range(groups):
                pieces = [
                    jnp.where(wanted == group * per + atom, 1.0, 0.0) for atom in range(per)
                ]
                chosen = chosen + dot(lesser[group], expand(pieces))
            outgoing[side, block] = chosen.astype(BF16)

    count = sum(there.astype(jnp.int32) for there, _ in links)
    pl.semaphore_wait(barrier, count)

    def edge_copy(side, block):
        return pltpu.make_async_remote_copy(
            src_ref=outgoing.at[side, block],
            dst_ref=lesser.at[groups + (1 - side) * edges + block],
            send_sem=edge_send.at[side, block],
            recv_sem=edge_recv.at[1 - side, block],
            device_id=links[side][1],
            device_id_type=MESH,
        )

    def arriving_edge(side, block):
        return pltpu.make_async_remote_copy(
            src_ref=outgoing.at[side, block],
            dst_ref=lesser.at[groups + side * edges + block],
            send_sem=edge_send.at[side, block],
            recv_sem=edge_recv.at[side, block],
            device_id=links[side][1],
            device_id_type=MESH,
        )

    def halo_copy(side, group):
        return pltpu.make_async_remote_copy(
            src_ref=halo.at[0, group],
            dst_ref=halo.at[2 - side, group],
            send_sem=halo_send.at[side],
            recv_sem=halo_recv.at[1 - side, group],
            device_id=links[2 + side][1],
            device_id_type=MESH,
        )

    def halo_sent(side):
        return pltpu.make_async_remote_copy(
            src_ref=halo.at[0],
            dst_ref=halo.at[2 - side],
            send_sem=halo_send.at[side],
            recv_sem=halo_recv.at[1 - side, 0],
            device_id=links[2 + side][1],
            device_id_type=MESH,
        )

    def arriving_halo(side, group):
        return pltpu.make_async_remote_copy(
            src_ref=halo.at[0, group],
            dst_ref=halo.at[1 + side, group],
            send_sem=halo_send.at[side],
            recv_sem=halo_recv.at[side, group],
            device_id=links[2 + side][1],
            device_id_type=MESH,
        )

    for side in range(2):
        @pl.when(links[side][0])
        def _():
            for block in range(edges):
                edge_copy(side, block).start()

    slots = -(-(atoms + 2 * edge) // 8) * 8
    blocks = groups + 2 * edges
    wide = 2 if groups % 2 == 0 else 1
    units = groups // wide

    def weigh(unit):
        for inner in range(wide):
            group = unit * wide + inner
            lanes = slice(inner * LANES, (inner + 1) * LANES)
            slot = iota((slots, LANES), 0)
            weights = jnp.zeros((slots, LANES), F32)
            for column in range(nbrs):
                atom_of = lane_values([neighbours[group * per + t, column] for t in range(per)])
                strength = lane_values([coupling[group * per + t, column] for t in range(per)])
                weights = weights + jnp.where(slot == atom_of, strength, 0.0)
            coarse = weights.astype(BF16).astype(F32)
            for level, part in enumerate((coarse, weights - coarse)):
                for block in range(blocks):
                    side = (block - groups) // edges
                    pieces = []
                    for t in range(per):
                        number = block * per + t if block < groups else ((block - groups) % edges) * per + t
                        at = number if block < groups else atoms + side * edge + number
                        known = block < groups or number < edge
                        pieces.append(part[at:at + 1, :] if known else jnp.zeros((1, LANES), F32))
                    mixing[unit, level, block, :, lanes] = expand(pieces)

    each(units, weigh)

    def joined(unit, first, last):
        value = None
        for start in range(first, last, 2):
            stop = min(start + 2, last)
            left = jnp.concatenate([lesser[block] for block in range(start, stop)], axis=1)
            for level in range(2):
                right = mixing[unit, level, start:stop].reshape((stop - start) * LANES, wide * LANES)
                term = dot(left, right)
                value = term if value is None else value + term
        return value

    def mix_own(unit):
        partial[unit] = joined(unit, 0, groups)

    each(units, mix_own)

    for side in range(2):
        @pl.when(links[side][0])
        def _():
            for block in range(edges):
                arriving_edge(side, block).wait_recv()

    def mix_border(unit):
        value = (partial[unit] + joined(unit, groups, blocks)).astype(BF16)
        for inner in range(wide):
            group = unit * wide + inner
            halo[0, group] = value[:, inner * LANES:(inner + 1) * LANES]
            for side in range(2):
                @pl.when(links[2 + side][0])
                def _():
                    halo_copy(side, group).start()

    each(units, mix_border)

    tall = (rows, LANES)
    same_atom = iota(square, 0) // rows == iota(square, 1) // rows
    for place, shift in enumerate((0, rows, -rows)):
        distance = iota(tall, 1) % rows - iota(tall, 0) + shift
        weight = jnp.zeros(tall, F32)
        for freq in range(freqs):
            weight = jnp.where(distance == offsets[freq], w_emit[freq], weight)
            weight = jnp.where(distance == -offsets[freq], w_absorb[freq], weight)
        full = jnp.concatenate([weight] * per, axis=0)
        full = jnp.where(same_atom, full, 0.0).astype(BF16)
        for inner in range(wide):
            for other in range(wide):
                band[place, inner * LANES:(inner + 1) * LANES, other * LANES:(other + 1) * LANES] = (
                    full if inner == other else jnp.zeros(square, BF16)
                )

    def neighbour(place, unit):
        return [halo[place, unit * wide + inner] for inner in range(wide)]

    def band_own(unit):
        partial[unit] = dot(jnp.concatenate(neighbour(0, unit), axis=1), band[0])

    each(units, band_own)

    def finish(unit):
        for inner in range(wide):
            group = unit * wide + inner
            for side in range(2):
                @pl.when(links[2 + side][0])
                def _():
                    arriving_halo(side, group).wait_recv()
            both = jnp.concatenate([halo[1, group], halo[2, group]], axis=1)
            sides = band[1:3, 0:LANES, 0:LANES].reshape(2 * LANES, LANES)
            value = partial[unit, :, inner * LANES:(inner + 1) * LANES] + dot(both, sides)
            total[group] = value.astype(BF16)
            product[group] = total[group].astype(F32)
            for row in range(ORB):
                source[group, row, 0:ORB, :] = (
                    source[group, row, 0:ORB, :] + product[group, row * ORB:(row + 1) * ORB, :]
                )
            refreshed[group] = sandwich(group)

    each(units, finish)

    for side in range(2):
        @pl.when(links[side][0])
        def _():
            for block in range(edges):
                edge_copy(side, block).wait_send()

        @pl.when(links[2 + side][0])
        def _():
            halo_sent(side).wait_send()


def finishing(rows, total, refreshed, sigma_out, g_out, sigma_near, g_near, written):
    per = LANES // rows
    square = (LANES, LANES)
    identity = jnp.where(iota(square, 0) == iota(square, 1), 1.0, 0.0).astype(BF16)
    copies = []
    for place, (values, near, out) in enumerate(((total, sigma_near, sigma_out), (refreshed, g_near, g_out))):
        for group in range(total.shape[0]):
            back = turned(identity, values[group]).astype(BF16)
            for atom in range(per):
                at = (group * per + atom) * PAIRS
                near[:, at:at + PAIRS] = back[atom * rows:(atom + 1) * rows, :]
        copies.append(pltpu.make_async_copy(near, out, written.at[place]))
        copies[-1].start()
    for copy in copies:
        copy.wait()


def compact(
    slabs, energies, rows, atoms, edge, nbrs, freqs,
    green_far, sigma_far, neighbours_far, coupling_far, down_far, up_far, offsets_far, emit_far, absorb_far,
    sigma_near, g_near,
    green, sigma_in, neighbours, coupling, send_down, send_up, offsets, w_emit, w_absorb, fetched,
    cut, across, source, product, lesser, partial, mixing, border, outgoing, arrived, halo, own_band, far_band,
    edge_send, edge_recv, halo_send, halo_recv, relay_send,
):
    per = LANES // rows
    groups = atoms // per
    last = groups - 1
    half = PAIRS // 2
    middle = LANES // 2
    span = groups * LANES
    fetches = [
        pltpu.make_async_copy(far, near, fetched.at[place])
        for place, (far, near) in enumerate((
            (green_far, green), (sigma_far, sigma_in), (down_far, send_down), (up_far, send_up),
            (neighbours_far, neighbours), (coupling_far, coupling),
            (offsets_far, offsets), (emit_far, w_emit), (absorb_far, w_absorb),
        ))
    ]
    for fetch in fetches:
        fetch.start()
    my_slab = lax.axis_index("slab")
    my_energy = lax.axis_index("energy")
    ahead = 1 - 2 * (my_energy % 2)
    odd = my_slab % 2 == 1
    even = jnp.logical_not(odd)
    exists = (my_slab > 0, my_slab < slabs - 1)
    relayed = odd
    beyond = my_energy - ahead
    inside = (beyond >= 0) & (beyond < energies)
    onward, origin = my_energy + 2 * ahead, my_energy - 2 * ahead
    relays = relayed & (onward >= 0) & (onward < energies)
    barrier = pltpu.get_barrier_semaphore()
    links = (
        (exists[0], {"slab": my_slab - 1}),
        (exists[1], {"slab": my_slab + 1}),
        (my_energy >= 0, {"energy": my_energy + ahead}),
        (inside, {"energy": beyond}),
    )
    greeted = list(links) + [(relayed & inside, {"energy": origin})]
    awaited = [there for there, _ in links] + [relays]
    for side in range(2):
        for energy, there in ((my_energy + ahead, exists[side]), (beyond, exists[side] & inside)):
            greeted.append((odd & there, {"energy": energy, "slab": my_slab + 2 * side - 1}))
            awaited.append(even & there)
    for there, target in greeted:
        @pl.when(there)
        def _():
            pl.semaphore_signal(barrier, inc=1, device_id=target, device_id_type=MESH)

    nothing = jnp.zeros((half, LANES), BF16)
    for side in range(2):
        @pl.when(jnp.logical_not(exists[side]))
        def _():
            for kind in range(3):
                arrived[side, kind] = nothing

    @pl.when(jnp.logical_not(inside))
    def _():
        for side in range(2):
            arrived[side, 2] = nothing
        for group in range(groups):
            halo[2, group] = jnp.zeros((PAIRS, LANES), BF16)

    spread = (ORB * PADDED, PAIRS)
    high, low = iota(spread, 0) // PADDED, iota(spread, 0) % PADDED
    swapped = jnp.where((low < ORB) & (iota(spread, 1) == low * ORB + high), 1.0, 0.0).astype(BF16)
    compacted = (PAIRS, PAIRS)
    straight = jnp.where(iota(compacted, 0) == iota(compacted, 1), 1.0, 0.0).astype(BF16)
    square = (LANES, LANES)

    def load(slot, blocks):
        stacked = jnp.concatenate([cut[0, block] for block in blocks], axis=0)
        across[slot] = turned(swapped, stacked).reshape(ORB, PADDED, LANES)
        stacked = jnp.concatenate([cut[1, block] for block in blocks], axis=0)
        source[slot] = turned(straight, stacked)

    def sandwich(slot):
        columns = []
        for column in range(ORB):
            left = across[slot, 0] * source[slot, column:column + 1, :]
            for inner in range(1, ORB):
                at = inner * ORB + column
                left = left + across[slot, inner] * source[slot, at:at + 1, :]
            columns.append(left)
        for column in range(ORB):
            right = columns[0] * across[slot, 0, column:column + 1, :]
            for inner in range(1, ORB):
                right = right + columns[inner] * across[slot, inner, column:column + 1, :]
            product[slot, pl.ds(column, ORB, stride=ORB), :] = right[:ORB, :]
        return product[slot]

    for fetch in fetches[:4]:
        fetch.wait()
    for place, ref in enumerate((green, sigma_in)):
        for atom in range(atoms):
            cut[place, atom] = ref[:, atom * PAIRS:(atom + 1) * PAIRS]

    load(groups, [send_down[0, t] for t in range(edge)] + [send_up[0, t] for t in range(edge)])
    edges = sandwich(groups)
    top, bottom = edges[:half], edges[half:]
    lower = iota((half, LANES), 1) < middle
    outgoing[0] = jnp.where(lower, top, pltpu.roll(bottom, middle, 1)).astype(BF16)
    outgoing[1] = jnp.where(lower, pltpu.roll(top, middle, 1), bottom).astype(BF16)

    count = sum(there.astype(jnp.int32) for there in awaited)

    def edge_copy(side, kind, slot):
        energy = (my_energy, my_energy + ahead, beyond)[kind]
        return pltpu.make_async_remote_copy(
            src_ref=outgoing.at[side],
            dst_ref=arrived.at[slot, kind],
            send_sem=edge_send.at[side],
            recv_sem=edge_recv.at[slot],
            device_id={"energy": energy, "slab": my_slab + 2 * side - 1},
            device_id_type=MESH,
        )

    def taking(side, kind, role):
        there = exists[side] if kind == 0 else exists[side] & role
        return there if kind < 2 else there & inside

    def edge_bytes(side, kinds):
        return pltpu.make_async_remote_copy(
            src_ref=arrived.at[side, 0:kinds],
            dst_ref=arrived.at[side, 0:kinds],
            send_sem=edge_send.at[side],
            recv_sem=edge_recv.at[side],
            device_id={"slab": my_slab + 2 * side - 1},
            device_id_type=MESH,
        )

    def counted(side, several, act):
        there = exists[side]
        for kinds, when in (
            (1, there & jnp.logical_not(several)),
            (2, there & several & jnp.logical_not(inside)),
            (3, there & several & inside),
        ):
            @pl.when(when)
            def _():
                act(edge_bytes(side, kinds))

    def halo_copy(kind, group):
        return pltpu.make_async_remote_copy(
            src_ref=halo.at[0, group],
            dst_ref=halo.at[1 + kind, group],
            send_sem=halo_send.at[kind],
            recv_sem=halo_recv.at[kind, group],
            device_id=links[2 + kind][1],
            device_id_type=MESH,
        )

    def relay_copy():
        return pltpu.make_async_remote_copy(
            src_ref=halo.at[1, last],
            dst_ref=halo.at[2, last],
            send_sem=relay_send,
            recv_sem=halo_recv.at[1, last],
            device_id={"energy": onward},
            device_id_type=MESH,
        )

    @pl.when(even)
    def _():
        pl.semaphore_wait(barrier, count)
        for kind in (2, 1, 0):
            for side in range(2):
                @pl.when(taking(side, kind, even))
                def _():
                    edge_copy(side, kind, 1 - side).start()

    for group in range(groups):
        load(group, range(group * per, (group + 1) * per))
    for group in range(groups):
        lesser[:, group * LANES:(group + 1) * LANES] = sandwich(group).astype(BF16)

    @pl.when(odd)
    def _():
        pl.semaphore_wait(barrier, count)
        for side in (1, 0):
            @pl.when(exists[side])
            def _():
                edge_copy(side, 0, 1 - side).start()

    for fetch in fetches[4:]:
        fetch.wait()
    slots = -(-(atoms + 2 * edge) // 8) * 8
    lane_atom = iota((1, span), 1) // rows

    def lane_values(values):
        result = jnp.full((1, span), values[0])
        for place in range(1, len(values)):
            result = jnp.where(lane_atom == place, values[place], result)
        return result

    slot_of = iota((slots, span), 0)
    weights = jnp.zeros((slots, span), F32)
    for column in range(nbrs):
        atom_of = lane_values([neighbours[atom, column] for atom in range(atoms)])
        strength = lane_values([coupling[atom, column] for atom in range(atoms)])
        weights = weights + jnp.where(slot_of == atom_of, strength, 0.0)
    tall = (rows, span)
    same_energy = iota(tall, 0) == iota(tall, 1) % rows

    def expanded(at):
        return jnp.where(same_energy, jnp.broadcast_to(weights[at:at + 1, :], tall), 0.0).astype(BF16)

    for atom in range(atoms):
        mixing[atom * rows:(atom + 1) * rows, :] = expanded(atom)
    empty = jnp.zeros((middle, span), BF16)
    for side in range(2):
        start = side * LANES
        for t in range(edge):
            part = expanded(atoms + side * edge + t)
            border[start + t * rows:start + (t + 1) * rows, 0:span] = part
            border[start + middle + t * rows:start + middle + (t + 1) * rows, span:2 * span] = part
        border[start:start + middle, span:2 * span] = empty
        border[start + middle:start + LANES, 0:span] = empty

    partial[...] = dot(lesser[...], mixing[...])

    def crossing(kind):
        value = dot(jnp.concatenate([arrived[0, kind], arrived[1, kind]], axis=1), border[...])
        return jnp.concatenate([value[:, 0:span], value[:, span:2 * span]], axis=0)

    def settle(mixed):
        for group in range(groups):
            halo[0, group] = mixed[:, group * LANES:(group + 1) * LANES].astype(BF16)

    @pl.when(even)
    def _():
        for side in range(2):
            @pl.when(exists[side])
            def _():
                edge_bytes(side, 1).wait_recv()

        settle(partial[...] + crossing(0))

    @pl.when(odd)
    def _():
        settle(partial[...])

    direct = jnp.logical_not(relayed)

    @pl.when(relayed)
    def _():
        halo_copy(0, last).start()

    for group in range(groups):
        @pl.when(inside if group < last else inside & direct)
        def _():
            halo_copy(1, group).start()

    for group in range(last):
        halo_copy(0, group).start()

    @pl.when(direct)
    def _():
        halo_copy(0, last).start()

    same_atom = iota(square, 0) // rows == iota(square, 1) // rows
    narrow = (rows, LANES)
    distance = iota(narrow, 1) % rows - iota(narrow, 0)
    near_weight = jnp.zeros(narrow, F32)
    ahead_weight = jnp.zeros(narrow, F32)
    behind_weight = jnp.zeros(narrow, F32)
    ahead_gap = rows - ahead * distance
    behind_gap = rows + ahead * distance
    upward = ahead > 0
    for freq in range(freqs):
        offset, emit, absorb = offsets[freq], w_emit[freq], w_absorb[freq]
        near_weight = jnp.where(distance == offset, emit, near_weight)
        near_weight = jnp.where(distance == -offset, absorb, near_weight)
        ahead_weight = jnp.where(ahead_gap == offset, jnp.where(upward, absorb, emit), ahead_weight)
        behind_weight = jnp.where(behind_gap == offset, jnp.where(upward, emit, absorb), behind_weight)

    def band(weight):
        return jnp.where(same_atom, jnp.concatenate([weight] * per, axis=0), 0.0).astype(BF16)

    own_band[...] = band(near_weight)
    far_band[0:LANES, :] = band(ahead_weight)
    far_band[LANES:2 * LANES, :] = band(behind_weight)
    for group in range(groups):
        partial[:, group * LANES:(group + 1) * LANES] = dot(halo[0, group], own_band[...])

    @pl.when(relayed)
    def _():
        halo_copy(0, last).wait_recv()

    @pl.when(relays)
    def _():
        relay_copy().start()

    @pl.when(odd)
    def _():
        for side in range(2):
            counted(side, odd, lambda copy: copy.wait_recv())

        pieces = [crossing(kind).astype(BF16) for kind in range(3)]
        for group in range(groups):
            lanes = slice(group * LANES, (group + 1) * LANES)
            far = jnp.concatenate([pieces[1][:, lanes], pieces[2][:, lanes]], axis=1)
            partial[:, lanes] = partial[:, lanes] + dot(pieces[0][:, lanes], own_band[...]) + dot(far, far_band[...])

    identity = jnp.where(iota(square, 0) == iota(square, 1), 1.0, 0.0).astype(BF16)

    def place_rows(near, group, values):
        back = turned(identity, values).astype(BF16)
        for atom in range(per):
            at = (group * per + atom) * PAIRS
            near[:, at:at + PAIRS] = back[atom * rows:(atom + 1) * rows, :]

    for group in range(groups):
        if group < last:
            halo_copy(0, group).wait_recv()
        else:
            @pl.when(direct)
            def _():
                halo_copy(0, last).wait_recv()

        @pl.when(inside)
        def _():
            halo_copy(1, group).wait_recv()

        both = jnp.concatenate([halo[1, group], halo[2, group]], axis=1)
        value = partial[:, group * LANES:(group + 1) * LANES] + dot(both, far_band[...])
        total = value.astype(BF16)
        place_rows(sigma_near, group, total)
        source[group] = source[group] + total.astype(F32)
        place_rows(g_near, group, sandwich(group).astype(BF16))

    for side in range(2):
        counted(side, even, lambda copy: copy.wait_send())

    def halo_bytes(kind, count):
        return pltpu.make_async_remote_copy(
            src_ref=halo.at[0, 0:count],
            dst_ref=halo.at[1 + kind, 0:count],
            send_sem=halo_send.at[kind],
            recv_sem=halo_recv.at[kind, 0],
            device_id=links[2 + kind][1],
            device_id_type=MESH,
        )

    halo_bytes(0, groups).wait_send()

    @pl.when(inside & direct)
    def _():
        halo_bytes(1, groups).wait_send()

    @pl.when(inside & relayed)
    def _():
        halo_bytes(1, last).wait_send()

    @pl.when(relays)
    def _():
        relay_copy().wait_send()


def delivering(sigma_near, g_near, sigma_out, g_out, written):
    copies = [
        pltpu.make_async_copy(near, out, written.at[place])
        for place, (near, out) in enumerate(((sigma_near, sigma_out), (g_near, g_out)))
    ]
    for copy in copies:
        copy.start()
    for copy in copies:
        copy.wait()


def on_device_compact(slabs, energies, green, sigma_in, *smalls):
    rows, flat = green.shape
    atoms = flat // PAIRS
    neighbours, _, send_down, _, offsets, _, _ = smalls
    edge = send_down.shape[1]
    per = LANES // rows
    groups = atoms // per
    span = groups * LANES
    vmem = pl.BlockSpec(memory_space=pltpu.VMEM)
    far = pl.BlockSpec(memory_space=pltpu.HBM)
    body = functools.partial(
        compact, slabs, energies, rows, atoms, edge, neighbours.shape[1], offsets.shape[0]
    )
    shape = jax.ShapeDtypeStruct((rows, flat), BF16)
    near_shape = pltpu.VMEM((rows, flat), BF16)
    near = pl.pallas_call(
        body,
        out_shape=(near_shape, near_shape),
        in_specs=[far] * 9,
        out_specs=(vmem, vmem),
        scratch_shapes=[
            pltpu.VMEM(green.shape, BF16),
            pltpu.VMEM(green.shape, BF16),
            *[pltpu.SMEM(small.shape, small.dtype) for small in smalls],
            pltpu.SemaphoreType.DMA((9,)),
            pltpu.VMEM((2, atoms, rows, PAIRS), BF16),
            pltpu.VMEM((groups + 1, ORB, PADDED, LANES), F32),
            pltpu.VMEM((groups + 1, PAIRS, LANES), F32),
            pltpu.VMEM((groups + 1, PAIRS, LANES), F32),
            pltpu.VMEM((PAIRS, span), BF16),
            pltpu.VMEM((PAIRS, span), F32),
            pltpu.VMEM((span, span), BF16),
            pltpu.VMEM((2 * LANES, 2 * span), BF16),
            pltpu.VMEM((2, PAIRS // 2, LANES), BF16),
            pltpu.VMEM((2, 3, PAIRS // 2, LANES), BF16),
            pltpu.VMEM((3, groups, PAIRS, LANES), BF16),
            pltpu.VMEM((LANES, LANES), BF16),
            pltpu.VMEM((2 * LANES, LANES), BF16),
            pltpu.SemaphoreType.DMA((2,)),
            pltpu.SemaphoreType.DMA((2,)),
            pltpu.SemaphoreType.DMA((2,)),
            pltpu.SemaphoreType.DMA((2, groups)),
            pltpu.SemaphoreType.DMA,
        ],
        compiler_params=pltpu.CompilerParams(
            collective_id=0, has_side_effects=True
        ),
    )(green, sigma_in, *smalls)
    return pl.pallas_call(
        delivering,
        out_shape=(shape, shape),
        in_specs=[vmem] * 2,
        out_specs=(far, far),
        scratch_shapes=[pltpu.SemaphoreType.DMA((2,))],
        compiler_params=pltpu.CompilerParams(vmem_limit_bytes=(4 + groups) << 20),
    )(*near)


def on_device(slabs, energies, green, sigma_in, neighbours, coupling, send_down, send_up, offsets, w_emit, w_absorb):
    rows, flat = green.shape
    atoms = flat // PAIRS
    edge = send_down.shape[1]
    per = LANES // rows
    groups = atoms // per
    edges = -(-edge // per)
    wide = 2 if groups % 2 == 0 else 1
    smalls = (neighbours, coupling, send_down, send_up, offsets, w_emit, w_absorb)
    if 2 * edge == per and groups == 2 and energies % 2 == 0:
        return on_device_compact(slabs, energies, green, sigma_in, *smalls)
    vmem = pl.BlockSpec(memory_space=pltpu.VMEM)
    far = pl.BlockSpec(memory_space=pltpu.HBM)
    body = functools.partial(
        kernel, slabs, energies, rows, atoms, edge, neighbours.shape[1], offsets.shape[0]
    )
    shape = jax.ShapeDtypeStruct((rows, flat), BF16)
    turned_shape = pltpu.VMEM((groups, PAIRS, LANES), BF16)
    total, refreshed = pl.pallas_call(
        body,
        out_shape=(turned_shape, turned_shape),
        in_specs=[far] * 9,
        out_specs=(vmem, vmem),
        scratch_shapes=[
            pltpu.VMEM(green.shape, BF16),
            pltpu.VMEM(green.shape, BF16),
            *[pltpu.SMEM(small.shape, small.dtype) for small in smalls],
            pltpu.SemaphoreType.DMA((9,)),
            pltpu.VMEM((groups, ORB, PADDED, LANES), F32),
            pltpu.VMEM((groups, ORB, PADDED, LANES), F32),
            pltpu.VMEM((groups, ORB, PADDED, LANES), F32),
            pltpu.VMEM((groups, PAIRS, LANES), F32),
            pltpu.VMEM((groups + 2 * edges, PAIRS, LANES), BF16),
            pltpu.VMEM((groups // wide, PAIRS, wide * LANES), F32),
            pltpu.VMEM((groups // wide, 2, groups + 2 * edges, LANES, wide * LANES), BF16),
            pltpu.VMEM((2, edges, PAIRS, LANES), BF16),
            pltpu.VMEM((3, groups, PAIRS, LANES), BF16),
            pltpu.VMEM((3, wide * LANES, wide * LANES), BF16),
            pltpu.SemaphoreType.DMA((2, edges)),
            pltpu.SemaphoreType.DMA((2, edges)),
            pltpu.SemaphoreType.DMA((2,)),
            pltpu.SemaphoreType.DMA((2, groups)),
        ],
        compiler_params=pltpu.CompilerParams(
            collective_id=0, has_side_effects=True
        ),
    )(green, sigma_in, *smalls)
    return pl.pallas_call(
        functools.partial(finishing, rows),
        out_shape=(shape, shape),
        in_specs=[vmem] * 2,
        out_specs=(far, far),
        scratch_shapes=[
            pltpu.VMEM((rows, flat), BF16),
            pltpu.VMEM((rows, flat), BF16),
            pltpu.SemaphoreType.DMA((2,)),
        ],
        compiler_params=pltpu.CompilerParams(vmem_limit_bytes=(4 + groups) << 20),
    )(total, refreshed)


def solution(mesh):
    placed = (
        P("energy", "slab"),
        P("energy", "slab"),
        P("slab", None),
        P("slab", None),
        P("slab", None),
        P("slab", None),
        P(),
        P(),
        P(),
    )
    return jax.shard_map(
        functools.partial(on_device, mesh.shape["slab"], mesh.shape["energy"]),
        mesh=mesh,
        in_specs=placed,
        out_specs=(P("energy", "slab"), P("energy", "slab")),
        check_vma=False,
    )
```

```python
import functools

import jax
import jax.numpy as jnp
from jax import lax
from jax.experimental import pallas as pl
from jax.experimental.pallas import tpu as pltpu
from jax.sharding import PartitionSpec as P

ORB = 12
PADDED = 16
PAIRS = ORB * ORB
LANES = 128
MESH = pl.DeviceIdType.MESH
F32 = jnp.float32
BF16 = jnp.bfloat16


def iota(shape, dim):
    return lax.broadcasted_iota(jnp.int32, shape, dim)


def turned(matrix, block):
    return lax.dot_general(matrix, block, (((1,), (1,)), ((), ())), preferred_element_type=F32)


def dot(left, right):
    return jnp.dot(left, right, preferred_element_type=F32)


def each(count, body):
    if count <= 2:
        for index in range(count):
            body(index)
    else:
        lax.fori_loop(0, count, lambda index, carry: (body(index), carry)[1], 0)


def kernel(
    slabs, energies, rows, atoms, edge, nbrs, freqs,
    green_far, sigma_far, neighbours_far, coupling_far, down_far, up_far, offsets_far, emit_far, absorb_far,
    total, refreshed,
    green, sigma_in, neighbours, coupling, send_down, send_up, offsets, w_emit, w_absorb, fetched,
    plain, across, source, product, lesser, partial, mixing, outgoing, halo, band,
    edge_send, edge_recv, halo_send, halo_recv,
):
    per = LANES // rows
    groups = atoms // per
    edges = outgoing.shape[1]
    fetches = [
        pltpu.make_async_copy(far, near, fetched.at[place])
        for place, (far, near) in enumerate((
            (green_far, green), (sigma_far, sigma_in), (down_far, send_down), (up_far, send_up),
            (neighbours_far, neighbours), (coupling_far, coupling),
            (offsets_far, offsets), (emit_far, w_emit), (absorb_far, w_absorb),
        ))
    ]
    for fetch in fetches:
        fetch.start()
    my_slab = lax.axis_index("slab")
    my_energy = lax.axis_index("energy")
    barrier = pltpu.get_barrier_semaphore()
    links = (
        (my_slab > 0, {"slab": my_slab - 1}),
        (my_slab < slabs - 1, {"slab": my_slab + 1}),
        (my_energy > 0, {"energy": my_energy - 1}),
        (my_energy < energies - 1, {"energy": my_energy + 1}),
    )
    for there, target in links:
        @pl.when(there)
        def _():
            pl.semaphore_signal(barrier, inc=1, device_id=target, device_id_type=MESH)

    for side in range(2):
        @pl.when(jnp.logical_not(links[side][0]))
        def _():
            for block in range(edges):
                lesser[groups + side * edges + block] = jnp.zeros((PAIRS, LANES), BF16)

        @pl.when(jnp.logical_not(links[2 + side][0]))
        def _():
            for block in range(groups):
                halo[1 + side, block] = jnp.zeros((PAIRS, LANES), BF16)

    spread = (ORB * PADDED, PAIRS)
    high, low = iota(spread, 0) // PADDED, iota(spread, 0) % PADDED
    real = low < ORB
    straight = jnp.where(real & (iota(spread, 1) == high * ORB + low), 1.0, 0.0).astype(BF16)
    swapped = jnp.where(real & (iota(spread, 1) == low * ORB + high), 1.0, 0.0).astype(BF16)
    square = (LANES, LANES)
    same_energy = iota(square, 0) % rows == iota(square, 1) % rows
    lane_atom = iota((1, LANES), 1) // rows

    fetches[0].wait()
    fetches[1].wait()

    def gathered(ref, group):
        pieces = [
            ref[:, (group * per + atom) * PAIRS:(group * per + atom + 1) * PAIRS]
            for atom in range(per)
        ]
        return jnp.concatenate(pieces, axis=0)

    for group in range(groups):
        stacked = gathered(green, group)
        plain[group] = turned(straight, stacked).reshape(ORB, PADDED, LANES)
        across[group] = turned(swapped, stacked).reshape(ORB, PADDED, LANES)
        source[group] = turned(straight, gathered(sigma_in, group)).reshape(ORB, PADDED, LANES)

    def sandwich(group):
        for row in range(ORB):
            left = plain[group, row, 0:1, :] * source[group, 0]
            for inner in range(1, ORB):
                left = left + plain[group, row, inner:inner + 1, :] * source[group, inner]
            right = left[0:1, :] * across[group, 0]
            for inner in range(1, ORB):
                right = right + left[inner:inner + 1, :] * across[group, inner]
            product[group, row * ORB:(row + 1) * ORB, :] = right[:ORB, :]
        return product[group].astype(BF16)

    def first(group):
        lesser[group] = sandwich(group)

    each(groups, first)
    for fetch in fetches[2:]:
        fetch.wait()

    def lane_values(values):
        result = jnp.full((1, LANES), values[0])
        for place in range(1, len(values)):
            result = jnp.where(lane_atom == place, values[place], result)
        return result

    def expand(pieces):
        full = jnp.concatenate([jnp.broadcast_to(piece, (rows, LANES)) for piece in pieces], axis=0)
        return jnp.where(same_energy, full, 0.0).astype(BF16)

    for side, sent in ((0, send_down), (1, send_up)):
        for block in range(edges):
            first_slot = block * per
            wanted = lane_values(
                [sent[0, first_slot + t] if first_slot + t < edge else jnp.int32(-1) for t in range(per)]
            )
            chosen = jnp.zeros((PAIRS, LANES), F32)
            for group in range(groups):
                pieces = [
                    jnp.where(wanted == group * per + atom, 1.0, 0.0) for atom in range(per)
                ]
                chosen = chosen + dot(lesser[group], expand(pieces))
            outgoing[side, block] = chosen.astype(BF16)

    count = sum(there.astype(jnp.int32) for there, _ in links)
    pl.semaphore_wait(barrier, count)

    def edge_copy(side, block):
        return pltpu.make_async_remote_copy(
            src_ref=outgoing.at[side, block],
            dst_ref=lesser.at[groups + (1 - side) * edges + block],
            send_sem=edge_send.at[side, block],
            recv_sem=edge_recv.at[1 - side, block],
            device_id=links[side][1],
            device_id_type=MESH,
        )

    def arriving_edge(side, block):
        return pltpu.make_async_remote_copy(
            src_ref=outgoing.at[side, block],
            dst_ref=lesser.at[groups + side * edges + block],
            send_sem=edge_send.at[side, block],
            recv_sem=edge_recv.at[side, block],
            device_id=links[side][1],
            device_id_type=MESH,
        )

    def halo_copy(side, group):
        return pltpu.make_async_remote_copy(
            src_ref=halo.at[0, group],
            dst_ref=halo.at[2 - side, group],
            send_sem=halo_send.at[side],
            recv_sem=halo_recv.at[1 - side, group],
            device_id=links[2 + side][1],
            device_id_type=MESH,
        )

    def halo_sent(side):
        return pltpu.make_async_remote_copy(
            src_ref=halo.at[0],
            dst_ref=halo.at[2 - side],
            send_sem=halo_send.at[side],
            recv_sem=halo_recv.at[1 - side, 0],
            device_id=links[2 + side][1],
            device_id_type=MESH,
        )

    def arriving_halo(side, group):
        return pltpu.make_async_remote_copy(
            src_ref=halo.at[0, group],
            dst_ref=halo.at[1 + side, group],
            send_sem=halo_send.at[side],
            recv_sem=halo_recv.at[side, group],
            device_id=links[2 + side][1],
            device_id_type=MESH,
        )

    for side in range(2):
        @pl.when(links[side][0])
        def _():
            for block in range(edges):
                edge_copy(side, block).start()

    slots = -(-(atoms + 2 * edge) // 8) * 8
    blocks = groups + 2 * edges
    wide = 2 if groups % 2 == 0 else 1
    units = groups // wide

    def weigh(unit):
        for inner in range(wide):
            group = unit * wide + inner
            lanes = slice(inner * LANES, (inner + 1) * LANES)
            slot = iota((slots, LANES), 0)
            weights = jnp.zeros((slots, LANES), F32)
            for column in range(nbrs):
                atom_of = lane_values([neighbours[group * per + t, column] for t in range(per)])
                strength = lane_values([coupling[group * per + t, column] for t in range(per)])
                weights = weights + jnp.where(slot == atom_of, strength, 0.0)
            coarse = weights.astype(BF16).astype(F32)
            for level, part in enumerate((coarse, weights - coarse)):
                for block in range(blocks):
                    side = (block - groups) // edges
                    pieces = []
                    for t in range(per):
                        number = block * per + t if block < groups else ((block - groups) % edges) * per + t
                        at = number if block < groups else atoms + side * edge + number
                        known = block < groups or number < edge
                        pieces.append(part[at:at + 1, :] if known else jnp.zeros((1, LANES), F32))
                    mixing[unit, level, block, :, lanes] = expand(pieces)

    each(units, weigh)

    def joined(unit, first, last):
        value = None
        for start in range(first, last, 2):
            stop = min(start + 2, last)
            left = jnp.concatenate([lesser[block] for block in range(start, stop)], axis=1)
            for level in range(2):
                right = mixing[unit, level, start:stop].reshape((stop - start) * LANES, wide * LANES)
                term = dot(left, right)
                value = term if value is None else value + term
        return value

    def mix_own(unit):
        partial[unit] = joined(unit, 0, groups)

    each(units, mix_own)

    for side in range(2):
        @pl.when(links[side][0])
        def _():
            for block in range(edges):
                arriving_edge(side, block).wait_recv()

    def mix_border(unit):
        value = (partial[unit] + joined(unit, groups, blocks)).astype(BF16)
        for inner in range(wide):
            group = unit * wide + inner
            halo[0, group] = value[:, inner * LANES:(inner + 1) * LANES]
            for side in range(2):
                @pl.when(links[2 + side][0])
                def _():
                    halo_copy(side, group).start()

    each(units, mix_border)

    tall = (rows, LANES)
    same_atom = iota(square, 0) // rows == iota(square, 1) // rows
    for place, shift in enumerate((0, rows, -rows)):
        distance = iota(tall, 1) % rows - iota(tall, 0) + shift
        weight = jnp.zeros(tall, F32)
        for freq in range(freqs):
            weight = jnp.where(distance == offsets[freq], w_emit[freq], weight)
            weight = jnp.where(distance == -offsets[freq], w_absorb[freq], weight)
        full = jnp.concatenate([weight] * per, axis=0)
        full = jnp.where(same_atom, full, 0.0).astype(BF16)
        for inner in range(wide):
            for other in range(wide):
                band[place, inner * LANES:(inner + 1) * LANES, other * LANES:(other + 1) * LANES] = (
                    full if inner == other else jnp.zeros(square, BF16)
                )

    def neighbour(place, unit):
        return [halo[place, unit * wide + inner] for inner in range(wide)]

    def band_own(unit):
        partial[unit] = dot(jnp.concatenate(neighbour(0, unit), axis=1), band[0])

    each(units, band_own)

    def finish(unit):
        for inner in range(wide):
            group = unit * wide + inner
            for side in range(2):
                @pl.when(links[2 + side][0])
                def _():
                    arriving_halo(side, group).wait_recv()
            both = jnp.concatenate([halo[1, group], halo[2, group]], axis=1)
            sides = band[1:3, 0:LANES, 0:LANES].reshape(2 * LANES, LANES)
            value = partial[unit, :, inner * LANES:(inner + 1) * LANES] + dot(both, sides)
            total[group] = value.astype(BF16)
            product[group] = total[group].astype(F32)
            for row in range(ORB):
                source[group, row, 0:ORB, :] = (
                    source[group, row, 0:ORB, :] + product[group, row * ORB:(row + 1) * ORB, :]
                )
            refreshed[group] = sandwich(group)

    each(units, finish)

    for side in range(2):
        @pl.when(links[side][0])
        def _():
            for block in range(edges):
                edge_copy(side, block).wait_send()

        @pl.when(links[2 + side][0])
        def _():
            halo_sent(side).wait_send()


def finishing(rows, total, refreshed, sigma_out, g_out, sigma_near, g_near, written):
    per = LANES // rows
    square = (LANES, LANES)
    identity = jnp.where(iota(square, 0) == iota(square, 1), 1.0, 0.0).astype(BF16)
    copies = []
    for place, (values, near, out) in enumerate(((total, sigma_near, sigma_out), (refreshed, g_near, g_out))):
        for group in range(total.shape[0]):
            back = turned(identity, values[group]).astype(BF16)
            for atom in range(per):
                at = (group * per + atom) * PAIRS
                near[:, at:at + PAIRS] = back[atom * rows:(atom + 1) * rows, :]
        copies.append(pltpu.make_async_copy(near, out, written.at[place]))
        copies[-1].start()
    for copy in copies:
        copy.wait()


def compact(
    slabs, energies, rows, atoms, edge, nbrs, freqs,
    green_far, sigma_far, neighbours_far, coupling_far, down_far, up_far, offsets_far, emit_far, absorb_far,
    sigma_near, g_near,
    green, sigma_in, neighbours, coupling, send_down, send_up, offsets, w_emit, w_absorb, fetched,
    cut, across, source, product, lesser, partial, mixing, border, outgoing, arrived, halo, own_band, far_band,
    edge_send, edge_recv, halo_send, halo_recv, relay_send,
):
    per = LANES // rows
    groups = atoms // per
    last = groups - 1
    half = PAIRS // 2
    middle = LANES // 2
    span = groups * LANES
    fetches = [
        pltpu.make_async_copy(far, near, fetched.at[place])
        for place, (far, near) in enumerate((
            (green_far, green), (sigma_far, sigma_in), (down_far, send_down), (up_far, send_up),
            (neighbours_far, neighbours), (coupling_far, coupling),
            (offsets_far, offsets), (emit_far, w_emit), (absorb_far, w_absorb),
        ))
    ]
    for fetch in fetches:
        fetch.start()
    my_slab = lax.axis_index("slab")
    my_energy = lax.axis_index("energy")
    ahead = 1 - 2 * (my_energy % 2)
    odd = my_slab % 2 == 1
    even = jnp.logical_not(odd)
    exists = (my_slab > 0, my_slab < slabs - 1)
    relayed = odd
    beyond = my_energy - ahead
    inside = (beyond >= 0) & (beyond < energies)
    onward, origin = my_energy + 2 * ahead, my_energy - 2 * ahead
    relays = relayed & (onward >= 0) & (onward < energies)
    barrier = pltpu.get_barrier_semaphore()
    links = (
        (exists[0], {"slab": my_slab - 1}),
        (exists[1], {"slab": my_slab + 1}),
        (my_energy >= 0, {"energy": my_energy + ahead}),
        (inside, {"energy": beyond}),
    )
    greeted = list(links) + [(relayed & inside, {"energy": origin})]
    awaited = [there for there, _ in links] + [relays]
    for side in range(2):
        for energy, there in ((my_energy + ahead, exists[side]), (beyond, exists[side] & inside)):
            greeted.append((odd & there, {"energy": energy, "slab": my_slab + 2 * side - 1}))
            awaited.append(even & there)
    for there, target in greeted:
        @pl.when(there)
        def _():
            pl.semaphore_signal(barrier, inc=1, device_id=target, device_id_type=MESH)

    nothing = jnp.zeros((half, LANES), BF16)
    for side in range(2):
        @pl.when(jnp.logical_not(exists[side]))
        def _():
            for kind in range(3):
                arrived[side, kind] = nothing

    @pl.when(jnp.logical_not(inside))
    def _():
        for side in range(2):
            arrived[side, 2] = nothing
        for group in range(groups):
            halo[2, group] = jnp.zeros((PAIRS, LANES), BF16)

    spread = (ORB * PADDED, PAIRS)
    high, low = iota(spread, 0) // PADDED, iota(spread, 0) % PADDED
    swapped = jnp.where((low < ORB) & (iota(spread, 1) == low * ORB + high), 1.0, 0.0).astype(BF16)
    compacted = (PAIRS, PAIRS)
    straight = jnp.where(iota(compacted, 0) == iota(compacted, 1), 1.0, 0.0).astype(BF16)
    square = (LANES, LANES)

    def load(slot, blocks):
        stacked = jnp.concatenate([cut[0, block] for block in blocks], axis=0)
        across[slot] = turned(swapped, stacked).reshape(ORB, PADDED, LANES)
        stacked = jnp.concatenate([cut[1, block] for block in blocks], axis=0)
        source[slot] = turned(straight, stacked)

    def sandwich(slot):
        columns = []
        for column in range(ORB):
            left = across[slot, 0] * source[slot, column:column + 1, :]
            for inner in range(1, ORB):
                at = inner * ORB + column
                left = left + across[slot, inner] * source[slot, at:at + 1, :]
            columns.append(left)
        for column in range(ORB):
            right = columns[0] * across[slot, 0, column:column + 1, :]
            for inner in range(1, ORB):
                right = right + columns[inner] * across[slot, inner, column:column + 1, :]
            product[slot, pl.ds(column, ORB, stride=ORB), :] = right[:ORB, :]
        return product[slot]

    for fetch in fetches[:4]:
        fetch.wait()
    for place, ref in enumerate((green, sigma_in)):
        for atom in range(atoms):
            cut[place, atom] = ref[:, atom * PAIRS:(atom + 1) * PAIRS]

    load(groups, [send_down[0, t] for t in range(edge)] + [send_up[0, t] for t in range(edge)])
    edges = sandwich(groups)
    top, bottom = edges[:half], edges[half:]
    lower = iota((half, LANES), 1) < middle
    outgoing[0] = jnp.where(lower, top, pltpu.roll(bottom, middle, 1)).astype(BF16)
    outgoing[1] = jnp.where(lower, pltpu.roll(top, middle, 1), bottom).astype(BF16)

    count = sum(there.astype(jnp.int32) for there in awaited)

    def edge_copy(side, kind, slot):
        energy = (my_energy, my_energy + ahead, beyond)[kind]
        return pltpu.make_async_remote_copy(
            src_ref=outgoing.at[side],
            dst_ref=arrived.at[slot, kind],
            send_sem=edge_send.at[side],
            recv_sem=edge_recv.at[slot],
            device_id={"energy": energy, "slab": my_slab + 2 * side - 1},
            device_id_type=MESH,
        )

    def taking(side, kind, role):
        there = exists[side] if kind == 0 else exists[side] & role
        return there if kind < 2 else there & inside

    def edge_bytes(side, kinds):
        return pltpu.make_async_remote_copy(
            src_ref=arrived.at[side, 0:kinds],
            dst_ref=arrived.at[side, 0:kinds],
            send_sem=edge_send.at[side],
            recv_sem=edge_recv.at[side],
            device_id={"slab": my_slab + 2 * side - 1},
            device_id_type=MESH,
        )

    def counted(side, several, act):
        there = exists[side]
        for kinds, when in (
            (1, there & jnp.logical_not(several)),
            (2, there & several & jnp.logical_not(inside)),
            (3, there & several & inside),
        ):
            @pl.when(when)
            def _():
                act(edge_bytes(side, kinds))

    def halo_copy(kind, group):
        return pltpu.make_async_remote_copy(
            src_ref=halo.at[0, group],
            dst_ref=halo.at[1 + kind, group],
            send_sem=halo_send.at[kind],
            recv_sem=halo_recv.at[kind, group],
            device_id=links[2 + kind][1],
            device_id_type=MESH,
        )

    def relay_copy():
        return pltpu.make_async_remote_copy(
            src_ref=halo.at[1, last],
            dst_ref=halo.at[2, last],
            send_sem=relay_send,
            recv_sem=halo_recv.at[1, last],
            device_id={"energy": onward},
            device_id_type=MESH,
        )

    @pl.when(even)
    def _():
        pl.semaphore_wait(barrier, count)
        for kind in (2, 1, 0):
            for side in range(2):
                @pl.when(taking(side, kind, even))
                def _():
                    edge_copy(side, kind, 1 - side).start()

    for group in range(groups):
        load(group, range(group * per, (group + 1) * per))
    for group in range(groups):
        lesser[:, group * LANES:(group + 1) * LANES] = sandwich(group).astype(BF16)

    @pl.when(odd)
    def _():
        pl.semaphore_wait(barrier, count)
        for side in (1, 0):
            @pl.when(exists[side])
            def _():
                edge_copy(side, 0, 1 - side).start()

    for fetch in fetches[4:]:
        fetch.wait()
    slots = -(-(atoms + 2 * edge) // 8) * 8
    lane_atom = iota((1, span), 1) // rows

    def lane_values(values):
        result = jnp.full((1, span), values[0])
        for place in range(1, len(values)):
            result = jnp.where(lane_atom == place, values[place], result)
        return result

    slot_of = iota((slots, span), 0)
    weights = jnp.zeros((slots, span), F32)
    for column in range(nbrs):
        atom_of = lane_values([neighbours[atom, column] for atom in range(atoms)])
        strength = lane_values([coupling[atom, column] for atom in range(atoms)])
        weights = weights + jnp.where(slot_of == atom_of, strength, 0.0)
    tall = (rows, span)
    same_energy = iota(tall, 0) == iota(tall, 1) % rows

    def expanded(at):
        return jnp.where(same_energy, jnp.broadcast_to(weights[at:at + 1, :], tall), 0.0).astype(BF16)

    for atom in range(atoms):
        mixing[atom * rows:(atom + 1) * rows, :] = expanded(atom)
    empty = jnp.zeros((middle, span), BF16)
    for side in range(2):
        start = side * LANES
        for t in range(edge):
            part = expanded(atoms + side * edge + t)
            border[start + t * rows:start + (t + 1) * rows, 0:span] = part
            border[start + middle + t * rows:start + middle + (t + 1) * rows, span:2 * span] = part
        border[start:start + middle, span:2 * span] = empty
        border[start + middle:start + LANES, 0:span] = empty

    partial[...] = dot(lesser[...], mixing[...])

    def crossing(kind):
        value = dot(jnp.concatenate([arrived[0, kind], arrived[1, kind]], axis=1), border[...])
        return jnp.concatenate([value[:, 0:span], value[:, span:2 * span]], axis=0)

    def settle(mixed):
        for group in range(groups):
            halo[0, group] = mixed[:, group * LANES:(group + 1) * LANES].astype(BF16)

    @pl.when(even)
    def _():
        for side in (1, 0):
            @pl.when(exists[side])
            def _():
                edge_bytes(side, 1).wait_recv()

            value = dot(arrived[side, 0], border[side * LANES:(side + 1) * LANES, :])
            value = partial[...] + jnp.concatenate([value[:, 0:span], value[:, span:2 * span]], axis=0)
            if side == 1:
                partial[...] = value
            else:
                settle(value)

    @pl.when(odd)
    def _():
        settle(partial[...])

    direct = jnp.logical_not(relayed)

    @pl.when(relayed)
    def _():
        halo_copy(0, last).start()

    for group in range(groups):
        @pl.when(inside if group < last else inside & direct)
        def _():
            halo_copy(1, group).start()

    for group in range(last):
        halo_copy(0, group).start()

    @pl.when(direct)
    def _():
        halo_copy(0, last).start()

    same_atom = iota(square, 0) // rows == iota(square, 1) // rows
    narrow = (rows, LANES)
    distance = iota(narrow, 1) % rows - iota(narrow, 0)
    near_weight = jnp.zeros(narrow, F32)
    ahead_weight = jnp.zeros(narrow, F32)
    behind_weight = jnp.zeros(narrow, F32)
    ahead_gap = rows - ahead * distance
    behind_gap = rows + ahead * distance
    upward = ahead > 0
    for freq in range(freqs):
        offset, emit, absorb = offsets[freq], w_emit[freq], w_absorb[freq]
        near_weight = jnp.where(distance == offset, emit, near_weight)
        near_weight = jnp.where(distance == -offset, absorb, near_weight)
        ahead_weight = jnp.where(ahead_gap == offset, jnp.where(upward, absorb, emit), ahead_weight)
        behind_weight = jnp.where(behind_gap == offset, jnp.where(upward, emit, absorb), behind_weight)

    def band(weight):
        return jnp.where(same_atom, jnp.concatenate([weight] * per, axis=0), 0.0).astype(BF16)

    own_band[...] = band(near_weight)
    far_band[0:LANES, :] = band(ahead_weight)
    far_band[LANES:2 * LANES, :] = band(behind_weight)
    for group in range(groups):
        partial[:, group * LANES:(group + 1) * LANES] = dot(halo[0, group], own_band[...])

    @pl.when(relayed)
    def _():
        halo_copy(0, last).wait_recv()

    @pl.when(relays)
    def _():
        relay_copy().start()

    @pl.when(odd)
    def _():
        for side in range(2):
            counted(side, odd, lambda copy: copy.wait_recv())

        pieces = [crossing(kind).astype(BF16) for kind in range(3)]
        for group in range(groups):
            lanes = slice(group * LANES, (group + 1) * LANES)
            far = jnp.concatenate([pieces[1][:, lanes], pieces[2][:, lanes]], axis=1)
            partial[:, lanes] = partial[:, lanes] + dot(pieces[0][:, lanes], own_band[...]) + dot(far, far_band[...])

    identity = jnp.where(iota(square, 0) == iota(square, 1), 1.0, 0.0).astype(BF16)

    def place_rows(near, group, values):
        back = turned(identity, values).astype(BF16)
        for atom in range(per):
            at = (group * per + atom) * PAIRS
            near[:, at:at + PAIRS] = back[atom * rows:(atom + 1) * rows, :]

    for group in range(groups):
        if group < last:
            halo_copy(0, group).wait_recv()
        else:
            @pl.when(direct)
            def _():
                halo_copy(0, last).wait_recv()

        @pl.when(inside)
        def _():
            halo_copy(1, group).wait_recv()

        both = jnp.concatenate([halo[1, group], halo[2, group]], axis=1)
        value = partial[:, group * LANES:(group + 1) * LANES] + dot(both, far_band[...])
        total = value.astype(BF16)
        place_rows(sigma_near, group, total)
        source[group] = source[group] + total.astype(F32)
        place_rows(g_near, group, sandwich(group).astype(BF16))

    for side in range(2):
        counted(side, even, lambda copy: copy.wait_send())

    def halo_bytes(kind, count):
        return pltpu.make_async_remote_copy(
            src_ref=halo.at[0, 0:count],
            dst_ref=halo.at[1 + kind, 0:count],
            send_sem=halo_send.at[kind],
            recv_sem=halo_recv.at[kind, 0],
            device_id=links[2 + kind][1],
            device_id_type=MESH,
        )

    halo_bytes(0, groups).wait_send()

    @pl.when(inside & direct)
    def _():
        halo_bytes(1, groups).wait_send()

    @pl.when(inside & relayed)
    def _():
        halo_bytes(1, last).wait_send()

    @pl.when(relays)
    def _():
        relay_copy().wait_send()


def delivering(sigma_near, g_near, sigma_out, g_out, written):
    copies = [
        pltpu.make_async_copy(near, out, written.at[place])
        for place, (near, out) in enumerate(((sigma_near, sigma_out), (g_near, g_out)))
    ]
    for copy in copies:
        copy.start()
    for copy in copies:
        copy.wait()


def on_device_compact(slabs, energies, green, sigma_in, *smalls):
    rows, flat = green.shape
    atoms = flat // PAIRS
    neighbours, _, send_down, _, offsets, _, _ = smalls
    edge = send_down.shape[1]
    per = LANES // rows
    groups = atoms // per
    span = groups * LANES
    vmem = pl.BlockSpec(memory_space=pltpu.VMEM)
    far = pl.BlockSpec(memory_space=pltpu.HBM)
    body = functools.partial(
        compact, slabs, energies, rows, atoms, edge, neighbours.shape[1], offsets.shape[0]
    )
    shape = jax.ShapeDtypeStruct((rows, flat), BF16)
    near_shape = pltpu.VMEM((rows, flat), BF16)
    near = pl.pallas_call(
        body,
        out_shape=(near_shape, near_shape),
        in_specs=[far] * 9,
        out_specs=(vmem, vmem),
        scratch_shapes=[
            pltpu.VMEM(green.shape, BF16),
            pltpu.VMEM(green.shape, BF16),
            *[pltpu.SMEM(small.shape, small.dtype) for small in smalls],
            pltpu.SemaphoreType.DMA((9,)),
            pltpu.VMEM((2, atoms, rows, PAIRS), BF16),
            pltpu.VMEM((groups + 1, ORB, PADDED, LANES), F32),
            pltpu.VMEM((groups + 1, PAIRS, LANES), F32),
            pltpu.VMEM((groups + 1, PAIRS, LANES), F32),
            pltpu.VMEM((PAIRS, span), BF16),
            pltpu.VMEM((PAIRS, span), F32),
            pltpu.VMEM((span, span), BF16),
            pltpu.VMEM((2 * LANES, 2 * span), BF16),
            pltpu.VMEM((2, PAIRS // 2, LANES), BF16),
            pltpu.VMEM((2, 3, PAIRS // 2, LANES), BF16),
            pltpu.VMEM((3, groups, PAIRS, LANES), BF16),
            pltpu.VMEM((LANES, LANES), BF16),
            pltpu.VMEM((2 * LANES, LANES), BF16),
            pltpu.SemaphoreType.DMA((2,)),
            pltpu.SemaphoreType.DMA((2,)),
            pltpu.SemaphoreType.DMA((2,)),
            pltpu.SemaphoreType.DMA((2, groups)),
            pltpu.SemaphoreType.DMA,
        ],
        compiler_params=pltpu.CompilerParams(
            collective_id=0, has_side_effects=True
        ),
    )(green, sigma_in, *smalls)
    return pl.pallas_call(
        delivering,
        out_shape=(shape, shape),
        in_specs=[vmem] * 2,
        out_specs=(far, far),
        scratch_shapes=[pltpu.SemaphoreType.DMA((2,))],
        compiler_params=pltpu.CompilerParams(vmem_limit_bytes=(4 + groups) << 20),
    )(*near)


def on_device(slabs, energies, green, sigma_in, neighbours, coupling, send_down, send_up, offsets, w_emit, w_absorb):
    rows, flat = green.shape
    atoms = flat // PAIRS
    edge = send_down.shape[1]
    per = LANES // rows
    groups = atoms // per
    edges = -(-edge // per)
    wide = 2 if groups % 2 == 0 else 1
    smalls = (neighbours, coupling, send_down, send_up, offsets, w_emit, w_absorb)
    if 2 * edge == per and groups == 2 and energies % 2 == 0:
        return on_device_compact(slabs, energies, green, sigma_in, *smalls)
    vmem = pl.BlockSpec(memory_space=pltpu.VMEM)
    far = pl.BlockSpec(memory_space=pltpu.HBM)
    body = functools.partial(
        kernel, slabs, energies, rows, atoms, edge, neighbours.shape[1], offsets.shape[0]
    )
    shape = jax.ShapeDtypeStruct((rows, flat), BF16)
    turned_shape = pltpu.VMEM((groups, PAIRS, LANES), BF16)
    total, refreshed = pl.pallas_call(
        body,
        out_shape=(turned_shape, turned_shape),
        in_specs=[far] * 9,
        out_specs=(vmem, vmem),
        scratch_shapes=[
            pltpu.VMEM(green.shape, BF16),
            pltpu.VMEM(green.shape, BF16),
            *[pltpu.SMEM(small.shape, small.dtype) for small in smalls],
            pltpu.SemaphoreType.DMA((9,)),
            pltpu.VMEM((groups, ORB, PADDED, LANES), F32),
            pltpu.VMEM((groups, ORB, PADDED, LANES), F32),
            pltpu.VMEM((groups, ORB, PADDED, LANES), F32),
            pltpu.VMEM((groups, PAIRS, LANES), F32),
            pltpu.VMEM((groups + 2 * edges, PAIRS, LANES), BF16),
            pltpu.VMEM((groups // wide, PAIRS, wide * LANES), F32),
            pltpu.VMEM((groups // wide, 2, groups + 2 * edges, LANES, wide * LANES), BF16),
            pltpu.VMEM((2, edges, PAIRS, LANES), BF16),
            pltpu.VMEM((3, groups, PAIRS, LANES), BF16),
            pltpu.VMEM((3, wide * LANES, wide * LANES), BF16),
            pltpu.SemaphoreType.DMA((2, edges)),
            pltpu.SemaphoreType.DMA((2, edges)),
            pltpu.SemaphoreType.DMA((2,)),
            pltpu.SemaphoreType.DMA((2, groups)),
        ],
        compiler_params=pltpu.CompilerParams(
            collective_id=0, has_side_effects=True
        ),
    )(green, sigma_in, *smalls)
    return pl.pallas_call(
        functools.partial(finishing, rows),
        out_shape=(shape, shape),
        in_specs=[vmem] * 2,
        out_specs=(far, far),
        scratch_shapes=[
            pltpu.VMEM((rows, flat), BF16),
            pltpu.VMEM((rows, flat), BF16),
            pltpu.SemaphoreType.DMA((2,)),
        ],
        compiler_params=pltpu.CompilerParams(vmem_limit_bytes=(4 + groups) << 20),
    )(total, refreshed)


def solution(mesh):
    placed = (
        P("energy", "slab"),
        P("energy", "slab"),
        P("slab", None),
        P("slab", None),
        P("slab", None),
        P("slab", None),
        P(),
        P(),
        P(),
    )
    return jax.shard_map(
        functools.partial(on_device, mesh.shape["slab"], mesh.shape["energy"]),
        mesh=mesh,
        in_specs=placed,
        out_specs=(P("energy", "slab"), P("energy", "slab")),
        check_vma=False,
    )
```
